256 devices in a mesh: probe: 2 (over x_lo), row: 16 (over x_hi, y, core), col: 8 (over z).
Axes of the slice: x: 4 (x_hi: 2, x_lo: 2; x = x_hi * 2 + x_lo), y: 4, z: 8, core: 2. Of those that a mesh axis runs over, the one named last changes fastest.
Arguments:
- flow_state: bfloat16 [2, 5, 192, 192, 384], P('probe', None, 'row', 'col'), may hold values from -6 to 6
- forcing: bfloat16 [2, 5, 192, 192, 384], P('probe', None, 'row', 'col'), may hold values from -6 to 6
- advect_x: bfloat16 [192, 192, 384], P('row', 'col'), may hold values from 0.19921875 to 1.5
- advect_y: bfloat16 [192, 192, 384], P('row', 'col'), may hold values from 0.19921875 to 1.5
- advect_z: bfloat16 [192, 192, 384], P('row', 'col'), may hold values from 0.19921875 to 1.5
- diffusivity: float32 [5], replicated, may hold values from 0.2 to 1
- deriv_x: bfloat16 [2, 384, 384], replicated, may hold values from -0.3125 to 0.3125
- deriv_y: bfloat16 [2, 192, 192], replicated, may hold values from -0.4375 to 0.4375
- deriv_z: bfloat16 [2, 192, 192], replicated, may hold values from -0.4375 to 0.4375
- test_mix: float32 [2, 2], replicated, may hold values from -4 to 4
Outputs:
- section_out: bfloat16 [2, 5, 192, 192, 384], P('probe', None, 'row', 'col')
- sketch: bfloat16 [2, 5, 192, 192, 384], P(None, None, 'row', 'col', 'probe')
The draws below stay inside these ranges and needn't reach their ends.
All inputs are finite; a program needn't handle non-finite values.
Results may differ from the reference program's by a relative error of at most 0.0095.
Values may be sent and summed in bfloat16 or wider, within the bound.
No kernel may reach another device: no remote copies, remote signals or barrier semaphores. Data moves between devices by JAX's collectives and lax.ppermute only.
A program may use at most 128 MiB of HBM per device.

```python
import math
import jax
import jax.numpy as jnp
from jax import lax

NX = 384
NY = 192
NZ = 192
VARS = 5
FRC_DEV = 1
FORCINGS = 2
N_PROBE = 2


def block_levels(rng, dims, cuts, low, largest):
    level, own = 1.0, jax.random.fold_in(rng, 6)
    for position, shards_of in cuts:
        steps = jnp.exp(jax.random.uniform(jax.random.fold_in(own, position), (shards_of,), jnp.float32, low / len(cuts), largest / len(cuts)))
        level = level * jnp.repeat(steps, dims[position] // shards_of).reshape([-1 if axis == position else 1 for axis in range(len(dims))])
    return level


def normal_values(rng, shape, scale, bound, shards=(), held_as=jnp.bfloat16):
    factor_of = block_levels(rng, shape, shards, -0.22, 0.18) if shards else 1.0
    result = jax.random.normal(rng, shape, jnp.float32) * scale * factor_of
    return jnp.minimum(jnp.maximum(result, -bound), bound).astype(held_as)


def setup_inputs(seed: int = 0) -> dict:
    seeds = jax.random.split(jax.random.key(seed), 11)
    return {
        "flow_state": normal_values(seeds[0], (FORCINGS, VARS, NY, NZ, NX), 1.0, 6.0, ((0, 2), (2, 16), (3, 8))),
        "forcing": normal_values(seeds[1], (FORCINGS, VARS, NY, NZ, NX), 1.0, 6.0, ((0, 2), (2, 16), (3, 8))),
        "advect_x": jnp.clip(0.19921875 + 1.3007812 * jax.random.uniform(seeds[2], (NY, NZ, NX), jnp.float32) ** block_levels(seeds[2], (NY, NZ, NX), ((0, 16), (1, 8)), -0.2, 0.2), 0.19921875, 1.5).astype(jnp.bfloat16),
        "advect_y": jnp.clip(0.19921875 + 1.3007812 * jax.random.uniform(seeds[3], (NY, NZ, NX), jnp.float32) ** block_levels(seeds[3], (NY, NZ, NX), ((0, 16), (1, 8)), -0.2, 0.2), 0.19921875, 1.5).astype(jnp.bfloat16),
        "advect_z": jnp.clip(0.19921875 + 1.3007812 * jax.random.uniform(seeds[4], (NY, NZ, NX), jnp.float32) ** block_levels(seeds[4], (NY, NZ, NX), ((0, 16), (1, 8)), -0.2, 0.2), 0.19921875, 1.5).astype(jnp.bfloat16),
        "diffusivity": jnp.clip(jnp.exp(jax.random.uniform(seeds[5], (VARS,), jnp.float32, math.log(0.2), math.log(1.0))), 0.2, 1.0),
        "deriv_x": normal_values(seeds[6], (2, NX, NX), NX ** -0.5, 0.3125),
        "deriv_y": normal_values(seeds[7], (2, NY, NY), NY ** -0.5, 0.4375),
        "deriv_z": normal_values(seeds[8], (2, NZ, NZ), NZ ** -0.5, 0.4375),
        "test_mix": normal_values(seeds[9], (FORCINGS, FORCINGS), FORCINGS ** -0.5, 4.0, (), jnp.float32),
    }


step_size = 0.25


def reference(flow_state, forcing, advect_x, advect_y, advect_z, diffusivity, deriv_x, deriv_y, deriv_z, test_mix):
    mat_x = deriv_x.astype(jnp.float32)
    mat_y = deriv_y.astype(jnp.float32)
    mat_z = deriv_z.astype(jnp.float32)
    vel_x = advect_x.astype(jnp.float32)
    vel_y = advect_y.astype(jnp.float32)
    vel_z = advect_z.astype(jnp.float32)
    sections = []
    for f in range(FORCINGS):
        per_var = []
        for v in range(VARS):
            field_f32 = flow_state[f, v].astype(jnp.float32)
            coeff = diffusivity[v]
            grad_x = jnp.einsum("yzj,kij->kyzi", field_f32, mat_x)
            term_x = -vel_x * grad_x[0] + coeff * grad_x[1]
            grad_y = jnp.einsum("jzx,kij->kizx", field_f32, mat_y)
            term_y = (-vel_y * grad_y[0] + coeff * grad_y[1]).astype(jnp.bfloat16)
            term_y = lax.optimization_barrier(term_y).astype(jnp.float32)
            grad_z = jnp.einsum("yjx,kij->kyix", field_f32, mat_z)
            term_z = (-vel_z * grad_z[0] + coeff * grad_z[1]).astype(jnp.bfloat16)
            term_z = lax.optimization_barrier(term_z).astype(jnp.float32)
            total_rhs = term_x + term_y + term_z + forcing[f, v].astype(jnp.float32)
            per_var.append((field_f32 + step_size * total_rhs).astype(jnp.bfloat16))
        sections.append(jnp.stack(per_var))
    section_out = jnp.stack(sections)
    columns = []
    for g in range(FORCINGS):
        summed = jnp.zeros(section_out.shape[1:], jnp.float32)
        for h in range(N_PROBE):
            group_sum = jnp.zeros(section_out.shape[1:], jnp.float32)
            for f in range(h * FRC_DEV, (h + 1) * FRC_DEV):
                group_sum = group_sum + section_out[f].astype(jnp.float32) * test_mix[f, g]
            rounded = lax.optimization_barrier(group_sum.astype(jnp.bfloat16))
            summed = summed + rounded.astype(jnp.float32)
        columns.append(summed.astype(jnp.bfloat16))
    sketch = jnp.stack(columns)
    return section_out, sketch
```

```python
import jax
import jax.numpy as jnp
import numpy as np
from jax import lax
from jax.experimental import pallas as pl
from jax.experimental.pallas import tpu as pltpu
from jax.sharding import PartitionSpec as P

step_size = 0.25

VMEM = pltpu.VMEM
F32 = jnp.float32
BF16 = jnp.bfloat16


def vspec():
    return pl.BlockSpec(memory_space=pltpu.VMEM)


def sspec():
    return pl.BlockSpec(memory_space=pltpu.SMEM)


def swap(x):
    return pltpu.roll(x, 64, x.ndim - 1)


def low_lanes(shape):
    return lax.broadcasted_iota(jnp.int32, shape, len(shape) - 1) < 64


def merge(half, first, second):
    low = low_lanes(first.shape)
    if half == 0:
        return jnp.where(low, first, swap(second))
    return jnp.where(low, swap(first), second)


def z_pack_kernel(state, adv, out):
    def body(a, carry):
        for yl in range(3):
            y = 3 * a + yl
            rows = [state[v, y].astype(F32) for v in range(5)] + [adv[y].astype(F32)]
            for b in range(2):
                for u in range(6):
                    at = yl * 216 + 24 * u
                    out[2 * a + b, at : at + 24, :] = rows[u][:, 256 * b : 256 * b + 128].astype(BF16)
                for q in range(3):
                    at = yl * 216 + 144 + 24 * q
                    tile = merge(b, rows[2 * q][:, 128:256], rows[2 * q + 1][:, 128:256])
                    out[2 * a + b, at : at + 24, :] = tile.astype(BF16)
        return carry

    lax.fori_loop(0, 4, body, 0)


def y_pack_kernel(state, adv, out):
    def lines(p, c):
        lanes = slice(128 * c, 128 * c + 128)
        if p < 2:
            block = state[2 * p : 2 * p + 2, :, :, lanes].astype(F32).reshape(24, 24, 128)
        else:
            block = jnp.concatenate([state[4, :, :, lanes], adv[:, :, lanes]], axis=0).astype(F32)
        return jnp.swapaxes(block, 0, 1)

    for p in range(3):
        for b in range(2):
            out[:, b, 72 * p : 72 * p + 72, :] = lines(p, 2 * b).reshape(8, 72, 128).astype(BF16)
    mid = [lines(p, 1) for p in range(2)]
    for b in range(2):
        tile = merge(b, mid[0], mid[1])
        out[:, b, 216:288, :] = tile.reshape(8, 72, 128).astype(BF16)
    last = lines(2, 1).reshape(8, 3, 24, 128)
    none = jnp.zeros((8, 24, 128), F32)
    for b in range(2):
        out[:, b, 288:312, :] = merge(b, last[:, 0], last[:, 1]).astype(BF16)
        out[:, b, 312:336, :] = merge(b, last[:, 2], none).astype(BF16)


def x_kernel(coef, state, forcing, adv, mat, out):
    lhs_mat = mat[...].reshape(768, 384)
    for v in range(5):
        for h in range(2):
            ys = slice(6 * h, 6 * h + 6)
            field = state[v, ys].astype(F32).reshape(144, 384)
            grad = lax.dot_general(
                field.astype(BF16), lhs_mat, (((1,), (1,)), ((), ())), preferred_element_type=F32
            )
            vel = adv[ys].astype(F32).reshape(144, 384)
            frc = forcing[v, ys].astype(F32).reshape(144, 384)
            term = coef[v] * grad[:, 384:] - vel * grad[:, :384]
            out[v, ys] = (field + step_size * (term + frc)).reshape(6, 24, 384)


def z_kernel(coef, recv, mat, out):
    lhs = mat[...].reshape(384, 192)
    low = low_lanes((192, 128))

    def tile(yl, t):
        at = yl * 216 + 24 * t
        return recv[:, at : at + 24, :].astype(F32).reshape(192, 128)

    def put(t, term):
        out[:, 24 * t : 24 * t + 24, :] = term.reshape(8, 24, 128).astype(BF16)

    tails = []
    for yl in range(3):
        tiles = [tile(yl, t) for t in range(9)]
        vel = tiles[5]
        vel_half = jnp.where(low, swap(tiles[8]), tiles[8])
        names = [0, 1, 2, 3, 4, 6, 7, 8]
        for n in range(0, 8, 2):
            rhs = jnp.concatenate([tiles[names[n]], tiles[names[n + 1]]], axis=1).astype(BF16)
            grad = jnp.dot(lhs, rhs, preferred_element_type=F32)
            for j in range(2):
                t = names[n + j]
                g0 = grad[:192, 128 * j : 128 * j + 128]
                g1 = grad[192:, 128 * j : 128 * j + 128]
                if t < 5:
                    put(yl * 7 + t, coef[t] * g1 - vel * g0)
                elif t < 8:
                    q = t - 6
                    c = jnp.where(low, coef[2 * q], coef[2 * q + 1])
                    put(yl * 7 + 5 + q, c * g1 - vel_half * g0)
                else:
                    tails.append(coef[4] * g1 - vel_half * g0)
    put(21, jnp.where(low, tails[0], swap(tails[1])))
    put(22, jnp.where(low, tails[2], 0.0))


def y_terms_kernel(coef, recv, mat, spread, gather, out, both):
    half = [spread[m] for m in range(2)]
    for k in range(2):
        acc = jnp.zeros((384, 384), F32)
        for m in range(2):
            left = jnp.dot(half[m], mat[k], preferred_element_type=F32).astype(BF16)
            acc = acc + lax.dot_general(
                left, half[m], (((1,), (1,)), ((), ())), preferred_element_type=F32
            )
        both[384 * k : 384 * k + 384, :] = acc.astype(BF16)
    lhs = both[...]
    take = gather[...]
    low = low_lanes((384, 128))
    member = lax.broadcasted_iota(jnp.int32, (16, 24, 128), 1).reshape(384, 128) >= 12

    def tile(t):
        return recv[:, 24 * t : 24 * t + 24, :].astype(F32).reshape(384, 128).astype(BF16)

    def put(t, term):
        out[:, 24 * t : 24 * t + 24, :] = term.reshape(16, 24, 128).astype(BF16)

    def coef_of(p):
        if p == 2:
            return jnp.where(member, 0.0, coef[4])
        return jnp.where(member, coef[2 * p + 1], coef[2 * p])

    vel_tail = jnp.dot(
        take, jnp.concatenate([tile(12), tile(13)], axis=1), preferred_element_type=F32
    )
    tail = [vel_tail[:, :128], vel_tail[:, 128:]]
    vel_half = [
        jnp.where(low, tail[0], swap(tail[0])),
        jnp.where(low, swap(tail[0]), tail[0]),
        jnp.where(low, tail[1], swap(tail[1])),
    ]

    def terms(t, vel, c):
        grad = jnp.dot(lhs, tile(t), preferred_element_type=F32)
        put(t, c * grad[384:] - vel * grad[:384])

    for zl in range(3):
        vel = jnp.dot(take, tile(6 + zl), preferred_element_type=F32)
        for p in range(3):
            terms(3 * p + zl, vel, coef_of(p))
        terms(9 + zl, vel_half[zl], jnp.where(low, coef_of(0), coef_of(1)))
    for j in range(2):
        terms(12 + j, tail[j], coef_of(2))


def join_kernel(probe, base, back_z, back_y, out, send, own, work):
    first = probe[0] == 0

    def put_lines(c, block):
        work[:, :, 128 * c : 128 * c + 128] = jnp.swapaxes(block, 0, 1)

    def y_tile(b, at, n):
        return back_y[:, b, at : at + 24 * n, :].astype(F32)

    low3 = low_lanes((24, 24, 128))
    low8 = low_lanes((8, 24, 128))
    low = low_lanes((24, 128))
    for p in range(3):
        for b in range(2):
            put_lines(2 * b, y_tile(b, 72 * p, 3).reshape(24, 24, 128))
        if p < 2:
            m = [y_tile(b, 216, 3).reshape(24, 24, 128) for b in range(2)]
            if p == 0:
                put_lines(1, jnp.where(low3, m[0], swap(m[1])))
            else:
                put_lines(1, jnp.where(low3, swap(m[0]), m[1]))
        else:
            m = [[y_tile(b, 288 + 24 * j, 1) for j in range(2)] for b in range(2)]
            parts = [
                jnp.where(low8, m[0][0], swap(m[1][0])),
                jnp.where(low8, swap(m[0][0]), m[1][0]),
                jnp.where(low8, m[0][1], swap(m[1][1])),
            ]
            put_lines(1, jnp.stack(parts, axis=1).reshape(24, 24, 128))
        for i in range(2 if p < 2 else 1):
            v = 2 * p + i

            def z_tile(d, t):
                return back_z[d, 24 * t : 24 * t + 24, :].astype(F32)

            def one(a, yl, v=v, i=i):
                y = 3 * a + yl
                full = [z_tile(2 * a + b, 7 * yl + v) for b in range(2)]
                if v < 4:
                    t, odd = 7 * yl + 5 + v // 2, v % 2
                else:
                    t, odd = 21 + yl // 2, yl % 2
                m = [z_tile(2 * a + b, t) for b in range(2)]
                if odd:
                    mid = jnp.where(low, swap(m[0]), m[1])
                else:
                    mid = jnp.where(low, m[0], swap(m[1]))
                res = []
                for c, part in enumerate((full[0], mid, full[1])):
                    lanes = slice(128 * c, 128 * c + 128)
                    total = base[v, y, :, lanes] + step_size * (part + work[12 * i + y, :, lanes])
                    total = total.astype(BF16)
                    out[v, y, :, lanes] = total
                    res.append(total.astype(F32))
                f = 12 * v + y
                send[f] = jnp.where(first, res[2], res[0]).astype(BF16)
                own[f] = jnp.where(first, res[0], res[2]).astype(BF16)
                return res[1]

            def body(a2, carry):
                mids = [one(2 * a2 + k // 3, k % 3) for k in range(6)]
                for j in range(3):
                    h = 60 + 6 * v + 3 * a2 + j
                    part0 = merge(0, mids[2 * j], mids[2 * j + 1])
                    part1 = merge(1, mids[2 * j], mids[2 * j + 1])
                    send[h] = jnp.where(first, part1, part0).astype(BF16)
                    own[h] = jnp.where(first, part0, part1).astype(BF16)
                return carry

            lax.fori_loop(0, 2, body, 0)


def sketch_kernel(probe, mix, own, recv, out):
    p = probe[0]
    low = low_lanes((24, 128))

    def body(i, carry):
        v = i // 6
        j = i % 6
        at = 12 * v + 2 * j
        for g in range(2):
            m_own = mix[p, g]
            m_recv = mix[1 - p, g]

            def mixed(n):
                a = (own[n].astype(F32) * m_own).astype(BF16).astype(F32)
                b = (recv[n].astype(F32) * m_recv).astype(BF16).astype(F32)
                return a + b

            half = mixed(60 + i)
            for k in range(2):
                full = mixed(at + k)
                piece = half if k == 0 else swap(half)
                turned = swap(full)
                head = jnp.where(p == 0, full, jnp.where(low, piece, turned))
                tail = jnp.where(p == 0, piece, turned)
                out[g, v, 2 * j + k, :, 0:128] = head.astype(BF16)
                out[g, v, 2 * j + k, :, 128:192] = tail[:, :64].astype(BF16)
        return carry

    lax.fori_loop(0, 30, body, 0)


def call(kernel, out_shapes, specs, scratch=(), name=None):
    many = isinstance(out_shapes, (list, tuple))
    return pl.pallas_call(
        kernel,
        out_shape=out_shapes,
        in_specs=specs,
        out_specs=[vspec() for _ in out_shapes] if many else vspec(),
        scratch_shapes=scratch,
        name=name,
    )


def row_tables():
    rows = np.arange(384)
    q = rows // 12
    point = 12 * (q // 2) + rows % 12
    spread = np.zeros((2, 384, 192), np.float32)
    spread[q % 2, rows, point] = 1.0
    gather = (spread[0] + spread[1]) @ spread[1].T
    return spread, gather


def on_device(
    flow_state,
    forcing,
    advect_x,
    advect_y,
    advect_z,
    diffusivity,
    deriv_x,
    deriv_y,
    deriv_z,
    test_mix,
):
    state = flow_state.reshape(5, 12, 24, 384)
    forced = forcing.reshape(5, 12, 24, 384)
    probe = lax.axis_index("probe").astype(jnp.int32).reshape(1)
    spread, gather = row_tables()
    spread = jnp.asarray(spread, BF16)
    gather = jnp.asarray(gather, BF16)

    def shape(s, t=BF16):
        return jax.ShapeDtypeStruct(s, t)

    to_z = call(z_pack_kernel, shape((8, 648, 128)), [vspec()] * 2, name="z_pack")(state, advect_z)
    at_z = lax.all_to_all(to_z, "col", split_axis=0, concat_axis=0, tiled=True)
    to_y = call(y_pack_kernel, shape((8, 2, 336, 128)), [vspec()] * 2, name="y_pack")(state, advect_y)
    at_y = lax.all_to_all(
        to_y.reshape(16, 336, 128), "row", split_axis=0, concat_axis=0, tiled=True
    )
    base = call(
        x_kernel, shape((5, 12, 24, 384), F32), [sspec()] + [vspec()] * 4, name="x_term"
    )(diffusivity, state, forced, advect_x, deriv_x)
    term_z = call(z_kernel, shape((8, 552, 128)), [sspec()] + [vspec()] * 2, name="z_term")(
        diffusivity, at_z, deriv_z
    )
    back_z = lax.all_to_all(term_z, "col", split_axis=0, concat_axis=0, tiled=True)
    term_y = call(
        y_terms_kernel,
        shape((16, 336, 128)),
        [sspec()] + [vspec()] * 4,
        [pltpu.VMEM((768, 384), BF16)],
        name="y_term",
    )(diffusivity, at_y, deriv_y, spread, gather)
    back_y = lax.all_to_all(term_y, "row", split_axis=0, concat_axis=0, tiled=True)
    section, send, own = call(
        join_kernel,
        [shape((5, 12, 24, 384)), shape((90, 24, 128)), shape((90, 24, 128))],
        [sspec()] + [vspec()] * 3,
        [pltpu.VMEM((24, 24, 384), F32)],
        name="join",
    )(probe, base, back_z, back_y.reshape(8, 2, 336, 128))
    recv = lax.ppermute(send, "probe", [(0, 1), (1, 0)])
    sketch = call(
        sketch_kernel, shape((2, 5, 12, 24, 192)), [sspec()] * 2 + [vspec()] * 2, name="sketch"
    )(probe, test_mix, own, recv)
    return (section[None], sketch)


def solution(mesh):
    placed = (
        P("probe", None, "row", "col", None),
        P("probe", None, "row", "col", None),
        P("row", "col", None),
        P("row", "col", None),
        P("row", "col", None),
        P(),
        P(),
        P(),
        P(),
        P(),
    )
    return jax.shard_map(
        on_device,
        mesh=mesh,
        in_specs=placed,
        out_specs=(P("probe", None, "row", "col", None), P(None, None, "row", "col", "probe")),
        check_vma=False,
    )
```

```python
import jax
import jax.numpy as jnp
import numpy as np
from jax import lax
from jax.experimental import pallas as pl
from jax.experimental.pallas import tpu as pltpu
from jax.sharding import PartitionSpec as P


step_size = 0.25


F32 = jnp.float32
BF16 = jnp.bfloat16


def vspec():
    return pl.BlockSpec(memory_space=pltpu.VMEM)


def sspec():
    return pl.BlockSpec(memory_space=pltpu.SMEM)


def swap(x):
    return pltpu.roll(x, 64, x.ndim - 1)


def low_lanes(shape):
    return lax.broadcasted_iota(jnp.int32, shape, len(shape) - 1) < 64


def merge(half, first, second):
    low = low_lanes(first.shape)
    if half == 0:
        return jnp.where(low, first, swap(second))
    return jnp.where(low, swap(first), second)


def z_pack_kernel(col, state, adv, *outs):
    me = col[0]
    for r in range(8):
        dest = lax.rem(me + r, 8)
        a = dest // 2

        def fill(b, r=r, a=a):
            def body(yl, carry):
                y = 3 * a + yl
                base = pl.multiple_of(yl * 216, 8)
                full = slice(256 * b, 256 * b + 128)
                for u in range(6):
                    src = state[u, y, :, full] if u < 5 else adv[y, :, full]
                    outs[r][pl.ds(base + 24 * u, 24), :] = src
                mid = [state[u, y, :, 128:256].astype(F32) for u in range(5)]
                mid.append(adv[y, :, 128:256].astype(F32))
                for q in range(3):
                    tile = merge(b, mid[2 * q], mid[2 * q + 1])
                    outs[r][pl.ds(base + 144 + 24 * q, 24), :] = tile.astype(BF16)
                return carry

            lax.fori_loop(0, 3, body, 0)

        @pl.when(lax.rem(dest, 2) == 0)
        def _():
            fill(0)

        @pl.when(lax.rem(dest, 2) == 1)
        def _():
            fill(1)


def y_pack_kernel(state, adv, out):
    def lines(p, c):
        lanes = slice(128 * c, 128 * c + 128)
        if p < 2:
            block = state[2 * p : 2 * p + 2, :, :, lanes].astype(F32).reshape(24, 24, 128)
        else:
            block = jnp.concatenate([state[4, :, :, lanes], adv[:, :, lanes]], axis=0).astype(F32)
        return jnp.swapaxes(block, 0, 1)

    for p in range(3):
        for b in range(2):
            out[:, b, 72 * p : 72 * p + 72, :] = lines(p, 2 * b).reshape(8, 72, 128).astype(BF16)
    mid = [lines(p, 1) for p in range(2)]
    for b in range(2):
        tile = merge(b, mid[0], mid[1])
        out[:, b, 216:288, :] = tile.reshape(8, 72, 128).astype(BF16)
    last = lines(2, 1).reshape(8, 3, 24, 128)
    none = jnp.zeros((8, 24, 128), F32)
    for b in range(2):
        out[:, b, 288:312, :] = merge(b, last[:, 0], last[:, 1]).astype(BF16)
        out[:, b, 312:336, :] = merge(b, last[:, 2], none).astype(BF16)


def x_kernel(coef, state, forcing, adv, mat, out):
    lhs_mat = mat[...].reshape(768, 384)
    for v in range(5):
        for h in range(2):
            ys = slice(6 * h, 6 * h + 6)
            field = state[v, ys].astype(F32).reshape(144, 384)
            grad = lax.dot_general(
                field.astype(BF16), lhs_mat, (((1,), (1,)), ((), ())), preferred_element_type=F32
            )
            vel = adv[ys].astype(F32).reshape(144, 384)
            frc = forcing[v, ys].astype(F32).reshape(144, 384)
            term = coef[v] * grad[:, 384:] - vel * grad[:, :384]
            out[v, ys] = (field + step_size * (term + frc)).reshape(6, 24, 384)


def z_kernel(col, coef, *refs):
    recv, mat, outs = refs[:8], refs[8], refs[9:]
    me = col[0]
    low = low_lanes((192, 128))
    point = lax.broadcasted_iota(jnp.int32, (192, 192), 0)
    place = lax.broadcasted_iota(jnp.int32, (192, 192), 1)
    block = jnp.zeros((192, 192), jnp.int32)
    for r in range(8):
        inside = (place >= 24 * r) & (place < 24 * r + 24)
        block = jnp.where(inside, 24 * lax.rem(me - r + 8, 8) - 24 * r, block)
    order = jnp.where(point == place + block, 1.0, 0.0).astype(BF16)
    parts = []
    for k in range(2):
        cols = jnp.dot(mat[k], order, preferred_element_type=F32).astype(BF16)
        rows = lax.dot_general(order, cols, (((0,), (0,)), ((), ())), preferred_element_type=F32)
        parts.append(rows.astype(BF16))
    lhs = jnp.concatenate(parts, axis=0)

    def tile(yl, t):
        at = yl * 216 + 24 * t
        return jnp.concatenate([ref[at : at + 24, :].astype(F32) for ref in recv], axis=0)

    def put(t, term):
        for r in range(8):
            outs[r][24 * t : 24 * t + 24, :] = term[24 * r : 24 * r + 24].astype(BF16)

    tails = []
    for yl in range(3):
        tiles = [tile(yl, t) for t in range(9)]
        vel = tiles[5]
        vel_half = jnp.where(low, swap(tiles[8]), tiles[8])
        names = [0, 1, 2, 3, 4, 6, 7, 8]
        for n in range(0, 8, 2):
            rhs = jnp.concatenate([tiles[names[n]], tiles[names[n + 1]]], axis=1).astype(BF16)
            grad = jnp.dot(lhs, rhs, preferred_element_type=F32)
            for j in range(2):
                t = names[n + j]
                g0 = grad[:192, 128 * j : 128 * j + 128]
                g1 = grad[192:, 128 * j : 128 * j + 128]
                if t < 5:
                    put(yl * 7 + t, coef[t] * g1 - vel * g0)
                elif t < 8:
                    q = t - 6
                    c = jnp.where(low, coef[2 * q], coef[2 * q + 1])
                    put(yl * 7 + 5 + q, c * g1 - vel_half * g0)
                else:
                    tails.append(coef[4] * g1 - vel_half * g0)
    put(21, jnp.where(low, tails[0], swap(tails[1])))
    put(22, jnp.where(low, tails[2], 0.0))


def y_terms_kernel(coef, recv, mat, spread, gather, out, both):
    half = [spread[m] for m in range(2)]
    for k in range(2):
        acc = jnp.zeros((384, 384), F32)
        for m in range(2):
            left = jnp.dot(half[m], mat[k], preferred_element_type=F32).astype(BF16)
            acc = acc + lax.dot_general(
                left, half[m], (((1,), (1,)), ((), ())), preferred_element_type=F32
            )
        both[384 * k : 384 * k + 384, :] = acc.astype(BF16)
    lhs = both[...]
    take = gather[...]
    low = low_lanes((384, 128))
    member = lax.broadcasted_iota(jnp.int32, (16, 24, 128), 1).reshape(384, 128) >= 12

    def tile(t):
        return recv[:, 24 * t : 24 * t + 24, :].astype(F32).reshape(384, 128).astype(BF16)

    def put(t, term):
        out[:, 24 * t : 24 * t + 24, :] = term.reshape(16, 24, 128).astype(BF16)

    def coef_of(p):
        if p == 2:
            return jnp.where(member, 0.0, coef[4])
        return jnp.where(member, coef[2 * p + 1], coef[2 * p])

    vel_tail = jnp.dot(
        take, jnp.concatenate([tile(12), tile(13)], axis=1), preferred_element_type=F32
    )
    tail = [vel_tail[:, :128], vel_tail[:, 128:]]
    vel_half = [
        jnp.where(low, tail[0], swap(tail[0])),
        jnp.where(low, swap(tail[0]), tail[0]),
        jnp.where(low, tail[1], swap(tail[1])),
    ]

    def terms(t, vel, c):
        grad = jnp.dot(lhs, tile(t), preferred_element_type=F32)
        put(t, c * grad[384:] - vel * grad[:384])

    for zl in range(3):
        vel = jnp.dot(take, tile(6 + zl), preferred_element_type=F32)
        for p in range(3):
            terms(3 * p + zl, vel, coef_of(p))
        terms(9 + zl, vel_half[zl], jnp.where(low, coef_of(0), coef_of(1)))
    for j in range(2):
        terms(12 + j, tail[j], coef_of(2))


def join_kernel(probe, col, base, back_y, *refs):
    arrivals, (out, send, own, work, back_z) = refs[:8], refs[8:]
    first = probe[0] == 0
    for r in range(8):
        back_z[lax.rem(col[0] + r, 8)] = arrivals[r][...]

    def put_lines(c, block):
        work[:, :, 128 * c : 128 * c + 128] = jnp.swapaxes(block, 0, 1)

    def y_tile(b, at, n):
        return back_y[:, b, at : at + 24 * n, :].astype(F32)

    low3 = low_lanes((24, 24, 128))
    low8 = low_lanes((8, 24, 128))
    low = low_lanes((24, 128))
    for p in range(3):
        for b in range(2):
            put_lines(2 * b, y_tile(b, 72 * p, 3).reshape(24, 24, 128))
        if p < 2:
            m = [y_tile(b, 216, 3).reshape(24, 24, 128) for b in range(2)]
            if p == 0:
                put_lines(1, jnp.where(low3, m[0], swap(m[1])))
            else:
                put_lines(1, jnp.where(low3, swap(m[0]), m[1]))
        else:
            m = [[y_tile(b, 288 + 24 * j, 1) for j in range(2)] for b in range(2)]
            parts = [
                jnp.where(low8, m[0][0], swap(m[1][0])),
                jnp.where(low8, swap(m[0][0]), m[1][0]),
                jnp.where(low8, m[0][1], swap(m[1][1])),
            ]
            put_lines(1, jnp.stack(parts, axis=1).reshape(24, 24, 128))
        for i in range(2 if p < 2 else 1):
            v = 2 * p + i

            def z_tile(d, t):
                return back_z[d, 24 * t : 24 * t + 24, :].astype(F32)

            def one(a, yl, v=v, i=i):
                y = 3 * a + yl
                full = [z_tile(2 * a + b, 7 * yl + v) for b in range(2)]
                if v < 4:
                    t, odd = 7 * yl + 5 + v // 2, v % 2
                else:
                    t, odd = 21 + yl // 2, yl % 2
                m = [z_tile(2 * a + b, t) for b in range(2)]
                if odd:
                    mid = jnp.where(low, swap(m[0]), m[1])
                else:
                    mid = jnp.where(low, m[0], swap(m[1]))
                res = []
                for c, part in enumerate((full[0], mid, full[1])):
                    lanes = slice(128 * c, 128 * c + 128)
                    total = base[v, y, :, lanes] + step_size * (part + work[12 * i + y, :, lanes])
                    total = total.astype(BF16)
                    out[v, y, :, lanes] = total
                    res.append(total.astype(F32))
                f = 12 * v + y
                send[f] = jnp.where(first, res[2], res[0]).astype(BF16)
                own[f] = jnp.where(first, res[0], res[2]).astype(BF16)
                return res[1]

            def body(a2, carry):
                mids = [one(2 * a2 + k // 3, k % 3) for k in range(6)]
                for j in range(3):
                    h = 60 + 6 * v + 3 * a2 + j
                    part0 = merge(0, mids[2 * j], mids[2 * j + 1])
                    part1 = merge(1, mids[2 * j], mids[2 * j + 1])
                    send[h] = jnp.where(first, part1, part0).astype(BF16)
                    own[h] = jnp.where(first, part0, part1).astype(BF16)
                return carry

            lax.fori_loop(0, 2, body, 0)


def sketch_kernel(probe, mix, own, recv, out):
    p = probe[0]
    low = low_lanes((24, 128))

    def body(i, carry):
        v = i // 6
        j = i % 6
        at = 12 * v + 2 * j
        for g in range(2):
            m_own = mix[p, g]
            m_recv = mix[1 - p, g]

            def mixed(n):
                a = (own[n].astype(F32) * m_own).astype(BF16).astype(F32)
                b = (recv[n].astype(F32) * m_recv).astype(BF16).astype(F32)
                return a + b

            half = mixed(60 + i)
            for k in range(2):
                full = mixed(at + k)
                piece = half if k == 0 else swap(half)
                turned = swap(full)
                head = jnp.where(p == 0, full, jnp.where(low, piece, turned))
                tail = jnp.where(p == 0, piece, turned)
                out[g, v, 2 * j + k, :, 0:128] = head.astype(BF16)
                out[g, v, 2 * j + k, :, 128:192] = tail[:, :64].astype(BF16)
        return carry

    lax.fori_loop(0, 30, body, 0)


def call(kernel, out_shapes, scalars, arrays, scratch=()):
    many = isinstance(out_shapes, (list, tuple))
    return pl.pallas_call(
        kernel,
        out_shape=out_shapes,
        in_specs=[sspec()] * len(scalars) + [vspec()] * len(arrays),
        out_specs=[vspec() for _ in out_shapes] if many else vspec(),
        scratch_shapes=scratch,
        compiler_params=pltpu.CompilerParams(vmem_limit_bytes=24 << 20),
    )(*scalars, *arrays)


def near(x):
    return pltpu.with_memory_space_constraint(x, pltpu.VMEM)


def shift(x, distance):
    return lax.ppermute(x, "col", [(i, (i + distance) % 8) for i in range(8)])


ROUTES = (3, 5, 4, 2, 6, 1, 7)


def row_tables():
    rows = np.arange(384)
    q = rows // 12
    point = 12 * (q // 2) + rows % 12
    spread = np.zeros((2, 384, 192), np.float32)
    spread[q % 2, rows, point] = 1.0
    gather = (spread[0] + spread[1]) @ spread[1].T
    return spread, gather


def on_device(
    flow_state,
    forcing,
    advect_x,
    advect_y,
    advect_z,
    diffusivity,
    deriv_x,
    deriv_y,
    deriv_z,
    test_mix,
):
    state = flow_state.reshape(5, 12, 24, 384)
    forced = forcing.reshape(5, 12, 24, 384)
    probe = lax.axis_index("probe").astype(jnp.int32).reshape(1)
    col = lax.axis_index("col").astype(jnp.int32).reshape(1)
    spread, gather = row_tables()
    spread = jnp.asarray(spread, BF16)
    gather = jnp.asarray(gather, BF16)

    def shape(s, t=BF16):
        return jax.ShapeDtypeStruct(s, t)

    def held(s, t=BF16):
        return pltpu.VMEM(s, t)

    to_y = call(y_pack_kernel, held((8, 2, 336, 128)), [], [state, advect_y])
    at_y = lax.all_to_all(
        to_y.reshape(16, 336, 128), "row", split_axis=0, concat_axis=0, tiled=True
    )
    to_z = call(z_pack_kernel, [held((648, 128))] * 8, [col], [state, advect_z])
    at_z = list(to_z)
    for r in ROUTES:
        at_z[r] = shift(to_z[r], r)
    base = call(
        x_kernel, held((5, 12, 24, 384), F32), [diffusivity], [state, forced, advect_x, deriv_x]
    )
    term_y = call(
        y_terms_kernel,
        held((16, 336, 128)),
        [diffusivity],
        [near(at_y), deriv_y, spread, gather],
        [pltpu.VMEM((768, 384), BF16)],
    )
    back_y = lax.all_to_all(term_y, "row", split_axis=0, concat_axis=0, tiled=True)
    term_z = call(
        z_kernel, [held((552, 128))] * 8, [col, diffusivity], [near(x) for x in at_z] + [deriv_z]
    )
    back_z = list(term_z)
    for r in ROUTES:
        back_z[r] = shift(term_z[r], -r)
    section, send, own = call(
        join_kernel,
        [shape((5, 12, 24, 384)), held((90, 24, 128)), held((90, 24, 128))],
        [probe, col],
        [near(base), near(back_y.reshape(8, 2, 336, 128))] + [near(x) for x in back_z],
        [pltpu.VMEM((24, 24, 384), F32), pltpu.VMEM((8, 552, 128), BF16)],
    )
    recv = lax.ppermute(send, "probe", [(0, 1), (1, 0)])
    sketch = call(
        sketch_kernel, shape((2, 5, 12, 24, 192)), [probe, test_mix], [near(own), near(recv)]
    )
    return (section[None], sketch)


def solution(mesh):
    placed = (
        P("probe", None, "row", "col", None),
        P("probe", None, "row", "col", None),
        P("row", "col", None),
        P("row", "col", None),
        P("row", "col", None),
        P(),
        P(),
        P(),
        P(),
        P(),
    )

    return jax.shard_map(
        on_device,
        mesh=mesh,
        in_specs=placed,
        out_specs=(P("probe", None, "row", "col", None), P(None, None, "row", "col", "probe")),
        check_vma=False,
    )
```

```python
import functools

import jax
import jax.numpy as jnp
from jax import lax
from jax.experimental import pallas as pl
from jax.experimental.pallas import tpu as pltpu
from jax.sharding import PartitionSpec as P


step_size = 0.25


F32 = jnp.float32
BF16 = jnp.bfloat16


def vspec():
    return pl.BlockSpec(memory_space=pltpu.VMEM)


def sspec():
    return pl.BlockSpec(memory_space=pltpu.SMEM)


def swap(x):
    return pltpu.roll(x, 64, x.ndim - 1)


def low_lanes(shape):
    return lax.broadcasted_iota(jnp.int32, shape, len(shape) - 1) < 64


def merge(half, first, second):
    low = low_lanes(first.shape)
    if half == 0:
        return jnp.where(low, first, swap(second))
    return jnp.where(low, swap(first), second)


def z_pack_kernel(col, state, adv, *outs):
    me = col[0]
    for r in range(8):
        dest = lax.rem(me + r, 8)
        a = dest // 2

        def fill(b, r=r, a=a):
            def body(yl, carry):
                y = 3 * a + yl
                base = pl.multiple_of(yl * 216, 8)
                full = slice(256 * b, 256 * b + 128)
                for u in range(6):
                    src = state[u, y, :, full] if u < 5 else adv[y, :, full]
                    outs[r][pl.ds(base + 24 * u, 24), :] = src
                mid = [state[u, y, :, 128:256].astype(F32) for u in range(5)]
                mid.append(adv[y, :, 128:256].astype(F32))
                for q in range(3):
                    tile = merge(b, mid[2 * q], mid[2 * q + 1])
                    outs[r][pl.ds(base + 144 + 24 * q, 24), :] = tile.astype(BF16)
                return carry

            lax.fori_loop(0, 3, body, 0)

        @pl.when(lax.rem(dest, 2) == 0)
        def _():
            fill(0)

        @pl.when(lax.rem(dest, 2) == 1)
        def _():
            fill(1)


def y_pack_kernel(state_far, adv_far, out, state, adv, sem):
    copies = [
        pltpu.make_async_copy(state_far.at[0:2], state.at[0:2], sem.at[0]),
        pltpu.make_async_copy(state_far.at[2:4], state.at[2:4], sem.at[1]),
        pltpu.make_async_copy(state_far.at[4], state.at[4], sem.at[2]),
        pltpu.make_async_copy(adv_far, adv, sem.at[3]),
    ]
    for copy in copies:
        copy.start()

    def lines(p, c):
        lanes = slice(128 * c, 128 * c + 128)
        if p < 2:
            block = state[2 * p : 2 * p + 2, :, :, lanes].astype(F32).reshape(24, 24, 128)
        else:
            block = jnp.concatenate([state[4, :, :, lanes], adv[:, :, lanes]], axis=0).astype(F32)
        return jnp.swapaxes(block, 0, 1)

    for p in range(3):
        for copy in copies[p : p + 1 if p < 2 else 4]:
            copy.wait()
        for b in range(2):
            out[:, b, 72 * p : 72 * p + 72, :] = lines(p, 2 * b).reshape(8, 72, 128).astype(BF16)
    mid = [lines(p, 1) for p in range(2)]
    for b in range(2):
        tile = merge(b, mid[0], mid[1])
        out[:, b, 216:288, :] = tile.reshape(8, 72, 128).astype(BF16)
    last = lines(2, 1).reshape(8, 3, 24, 128)
    none = jnp.zeros((8, 24, 128), F32)
    for b in range(2):
        out[:, b, 288:312, :] = merge(b, last[:, 0], last[:, 1]).astype(BF16)
        out[:, b, 312:336, :] = merge(b, last[:, 2], none).astype(BF16)


def xy_kernel(coef, state, forcing, adv, mat, back_y, out, work):
    lhs_mat = mat[...].reshape(768, 384)
    low3 = low_lanes((24, 24, 128))
    low8 = low_lanes((8, 24, 128))

    def put_lines(c, block):
        work[:, :, 128 * c : 128 * c + 128] = jnp.swapaxes(block, 0, 1)

    def y_tile(b, at, n):
        return back_y[:, b, at : at + 24 * n, :].astype(F32)

    for p in range(3):
        for b in range(2):
            put_lines(2 * b, y_tile(b, 72 * p, 3).reshape(24, 24, 128))
        if p < 2:
            m = [y_tile(b, 216, 3).reshape(24, 24, 128) for b in range(2)]
            if p == 0:
                put_lines(1, jnp.where(low3, m[0], swap(m[1])))
            else:
                put_lines(1, jnp.where(low3, swap(m[0]), m[1]))
        else:
            m = [[y_tile(b, 288 + 24 * j, 1) for j in range(2)] for b in range(2)]
            parts = [
                jnp.where(low8, m[0][0], swap(m[1][0])),
                jnp.where(low8, swap(m[0][0]), m[1][0]),
                jnp.where(low8, m[0][1], swap(m[1][1])),
            ]
            put_lines(1, jnp.stack(parts, axis=1).reshape(24, 24, 128))
        for i in range(2 if p < 2 else 1):
            v = 2 * p + i
            for h in range(2):
                ys = slice(6 * h, 6 * h + 6)
                field = state[v, ys].astype(F32).reshape(144, 384)
                grad = lax.dot_general(
                    field.astype(BF16),
                    lhs_mat,
                    (((1,), (1,)), ((), ())),
                    preferred_element_type=F32,
                )
                vel = adv[ys].astype(F32).reshape(144, 384)
                frc = forcing[v, ys].astype(F32).reshape(144, 384)
                term = coef[v] * grad[:, 384:] - vel * grad[:, :384]
                term = term + work[12 * i + 6 * h : 12 * i + 6 * h + 6].reshape(144, 384)
                out[v, ys] = (field + step_size * (term + frc)).reshape(6, 24, 384)


def matrices_kernel(col, mat_y, mat_z, lines_y, lines_z):
    me = col[0]
    point = lax.broadcasted_iota(jnp.int32, (192, 192), 0)
    place = lax.broadcasted_iota(jnp.int32, (192, 192), 1)
    block = jnp.zeros((192, 192), jnp.int32)
    for r in range(8):
        inside = (place >= 24 * r) & (place < 24 * r + 24)
        block = jnp.where(inside, 24 * lax.rem(me - r + 8, 8) - 24 * r, block)
    order = jnp.where(point == place + block, 1.0, 0.0).astype(BF16)
    for k in range(2):
        cols = jnp.dot(mat_z[k], order, preferred_element_type=F32).astype(BF16)
        rows = lax.dot_general(order, cols, (((0,), (0,)), ((), ())), preferred_element_type=F32)
        lines_z[192 * k : 192 * k + 192, :] = rows.astype(BF16)

    def spots(index):
        q = lax.shift_right_logical(index * 5462, 16)
        return lax.rem(q, 2), 12 * lax.shift_right_logical(q, 1) + index - 12 * q

    member, line = spots(lax.broadcasted_iota(jnp.int32, (384, 192), 0))
    same = line == lax.broadcasted_iota(jnp.int32, (384, 192), 1)
    spread = [jnp.where(same & (member == m), 1.0, 0.0).astype(BF16) for m in range(2)]
    for k in range(2):
        acc = jnp.zeros((384, 384), F32)
        for m in range(2):
            left = jnp.dot(spread[m], mat_y[k], preferred_element_type=F32).astype(BF16)
            acc = acc + lax.dot_general(
                left, spread[m], (((1,), (1,)), ((), ())), preferred_element_type=F32
            )
        lines_y[384 * k : 384 * k + 384, :] = acc.astype(BF16)
    line_to = spots(lax.broadcasted_iota(jnp.int32, (384, 384), 0))[1]
    member_from, line_from = spots(lax.broadcasted_iota(jnp.int32, (384, 384), 1))
    pick = (line_to == line_from) & (member_from == 1)
    lines_y[768:1152, :] = jnp.where(pick, 1.0, 0.0).astype(BF16)


def z_kernel(coef, *refs):
    recv, lines, outs = refs[:8], refs[8], refs[9:]
    low = low_lanes((192, 128))
    lhs = lines[...]

    def tile(yl, t):
        at = yl * 216 + 24 * t
        return jnp.concatenate([ref[at : at + 24, :].astype(F32) for ref in recv], axis=0)

    def put(t, term):
        for r in range(8):
            outs[r][24 * t : 24 * t + 24, :] = term[24 * r : 24 * r + 24].astype(BF16)

    tails = []
    for yl in range(3):
        tiles = [tile(yl, t) for t in range(9)]
        vel = tiles[5]
        vel_half = jnp.where(low, swap(tiles[8]), tiles[8])
        names = [0, 1, 2, 3, 4, 6, 7, 8]
        for n in range(0, 8, 2):
            rhs = jnp.concatenate([tiles[names[n]], tiles[names[n + 1]]], axis=1).astype(BF16)
            grad = jnp.dot(lhs, rhs, preferred_element_type=F32)
            for j in range(2):
                t = names[n + j]
                g0 = grad[:192, 128 * j : 128 * j + 128]
                g1 = grad[192:, 128 * j : 128 * j + 128]
                if t < 5:
                    put(yl * 7 + t, coef[t] * g1 - vel * g0)
                elif t < 8:
                    q = t - 6
                    c = jnp.where(low, coef[2 * q], coef[2 * q + 1])
                    put(yl * 7 + 5 + q, c * g1 - vel_half * g0)
                else:
                    tails.append(coef[4] * g1 - vel_half * g0)
    put(21, jnp.where(low, tails[0], swap(tails[1])))
    put(22, jnp.where(low, tails[2], 0.0))


def y_kernel(coef, recv, lines, out):
    lhs = lines[0:768, :]
    take = lines[768:1152, :]
    low = low_lanes((384, 128))
    member = lax.broadcasted_iota(jnp.int32, (16, 24, 128), 1).reshape(384, 128) >= 12

    def tile(t):
        return recv[:, 24 * t : 24 * t + 24, :].astype(F32).reshape(384, 128).astype(BF16)

    def put(t, term):
        out[:, 24 * t : 24 * t + 24, :] = term.reshape(16, 24, 128).astype(BF16)

    def coef_of(p):
        if p == 2:
            return jnp.where(member, 0.0, coef[4])
        return jnp.where(member, coef[2 * p + 1], coef[2 * p])

    vel_tail = jnp.dot(
        take, jnp.concatenate([tile(12), tile(13)], axis=1), preferred_element_type=F32
    )
    tail = [vel_tail[:, :128], vel_tail[:, 128:]]
    vel_half = [
        jnp.where(low, tail[0], swap(tail[0])),
        jnp.where(low, swap(tail[0]), tail[0]),
        jnp.where(low, tail[1], swap(tail[1])),
    ]

    work = [(12, tail[0], coef_of(2)), (13, tail[1], coef_of(2))]
    vel_full = jnp.dot(
        take, jnp.concatenate([tile(6), tile(7)], axis=1), preferred_element_type=F32
    )
    vels = [vel_full[:, :128], vel_full[:, 128:]]
    vels.append(jnp.dot(take, tile(8), preferred_element_type=F32))
    for zl in range(3):
        work += [(3 * p + zl, vels[zl], coef_of(p)) for p in range(3)]
        work.append((9 + zl, vel_half[zl], jnp.where(low, coef_of(0), coef_of(1))))
    for n in range(0, 14, 2):
        pair = work[n : n + 2]
        rhs = jnp.concatenate([tile(t) for t, _, _ in pair], axis=1)
        grad = jnp.dot(lhs, rhs, preferred_element_type=F32)
        for k, (t, vel, c) in enumerate(pair):
            lanes = slice(128 * k, 128 * k + 128)
            put(t, c * grad[384:, lanes] - vel * grad[:384, lanes])


def tiles_of(p):
    return 36 if p < 2 else 20


def join_kernel(p, probe, col, *refs):
    count = 2 if p < 2 else 1
    base, arrivals = refs[0], refs[1:9]
    out, send, own, rows, sem = refs[-5:]
    first = probe[0] == 0
    me = col[0]
    low = low_lanes((24, 128))

    def give(n, half0, half1):
        send[n] = jnp.where(first, half1, half0).astype(BF16)
        own[n] = jnp.where(first, half0, half1).astype(BF16)

    def fill(odd_me):
        for k in range(4):
            r = [(2 * k - odd_me) % 8, (2 * k - odd_me + 1) % 8]
            a = lax.rem(me + r[0], 8) // 2

            def z_tile(b, t, r=r):
                return arrivals[r[b]][24 * t : 24 * t + 24, :].astype(F32)

            mids = []
            for yl in range(3):
                y = 3 * a + yl
                for i in range(count):
                    v = 2 * p + i
                    full = [z_tile(b, 7 * yl + v) for b in range(2)]
                    t, odd = (7 * yl + 5 + p, i) if p < 2 else (21 + yl // 2, yl % 2)
                    m = [z_tile(b, t) for b in range(2)]
                    if odd:
                        mid = jnp.where(low, swap(m[0]), m[1])
                    else:
                        mid = jnp.where(low, m[0], swap(m[1]))
                    res = []
                    for c, part in enumerate((full[0], mid, full[1])):
                        lanes = slice(128 * c, 128 * c + 128)
                        total = (base[v, y, :, lanes] + step_size * part).astype(BF16)
                        rows[i, y, :, lanes] = total
                        res.append(total.astype(F32))
                    give(12 * i + y, res[0], res[2])
                    mids.append(res[1])
                if p < 2:
                    pair = mids[-2:]
                    give(24 + y, merge(0, *pair), merge(1, *pair))
            if p == 2:
                none = jnp.zeros((24, 128), F32)
                give(12 + a, merge(0, mids[0], mids[1]), merge(1, mids[0], mids[1]))
                give(16 + a, merge(0, mids[2], none), merge(1, mids[2], none))

    for odd_me in range(2):

        @pl.when(lax.rem(me, 2) == odd_me)
        def _(odd_me=odd_me):
            fill(odd_me)

    copies = [
        pltpu.make_async_copy(rows.at[i], out.at[2 * p + i], sem.at[i]) for i in range(count)
    ]
    for copy in copies:
        copy.start()
    for copy in copies:
        copy.wait()


def sketch_kernel(q, probe, mix, *refs):
    count = 2 if q < 2 else 1
    own, recv = refs[:2]
    out, rows, sem = refs[-3:]
    p = probe[0]
    low = low_lanes((24, 128))

    def mixed(n, g):
        a = (own[n].astype(F32) * mix[p, g]).astype(BF16).astype(F32)
        b = (recv[n].astype(F32) * mix[1 - p, g]).astype(BF16).astype(F32)
        return a + b

    def put(i, g, y, full, piece):
        turned = swap(full)
        head = jnp.where(p == 0, full, jnp.where(low, piece, turned))
        tail = jnp.where(p == 0, piece, turned)
        rows[i, g, y, :, 0:128] = head.astype(BF16)
        rows[i, g, y, :, 128:192] = tail[:, :64].astype(BF16)

    def body(a, carry):
        for g in range(2):
            for yl in range(3):
                y = 3 * a + yl
                if q < 2:
                    half = mixed(24 + y, g)
                    put(0, g, y, mixed(y, g), half)
                    put(1, g, y, mixed(12 + y, g), swap(half))
                else:
                    half = mixed(12 + a if yl < 2 else 16 + a, g)
                    put(0, g, y, mixed(y, g), swap(half) if yl == 1 else half)
        return carry

    lax.fori_loop(0, 4, body, 0)
    copies = [
        pltpu.make_async_copy(rows.at[i, g], out.at[g, 2 * q + i], sem.at[i, g])
        for i in range(count)
        for g in range(2)
    ]
    for copy in copies:
        copy.start()
    for copy in copies:
        copy.wait()


def call(kernel, out_shapes, scalars, arrays, scratch=(), kept=(), spaces=None, stay=False):
    many = isinstance(out_shapes, (list, tuple))
    specs = spaces or [vspec() for _ in (out_shapes if many else [0])]
    before = len(scalars) + len(arrays)
    return pl.pallas_call(
        kernel,
        out_shape=out_shapes,
        in_specs=[sspec()] * len(scalars)
        + [pl.BlockSpec(memory_space=pl.ANY) if stay else vspec()] * len(arrays)
        + [pl.BlockSpec(memory_space=pl.ANY)] * len(kept),
        out_specs=specs if many else specs[0],
        scratch_shapes=scratch,
        input_output_aliases={before + n: n for n in range(len(kept))},
        compiler_params=pltpu.CompilerParams(vmem_limit_bytes=16 << 20),
    )(*scalars, *arrays, *kept)


def far(x):
    return pltpu.with_memory_space_constraint(x, pltpu.HBM)


def near(x):
    return pltpu.with_memory_space_constraint(x, pltpu.VMEM)


def shift(x, distance):
    return lax.ppermute(x, "col", [(i, (i + distance) % 8) for i in range(8)])


ROUTES = (3, 5, 4, 2, 6, 1, 7)


def on_device(
    flow_state,
    forcing,
    advect_x,
    advect_y,
    advect_z,
    diffusivity,
    deriv_x,
    deriv_y,
    deriv_z,
    test_mix,
):
    state = flow_state.reshape(5, 12, 24, 384)
    forced = forcing.reshape(5, 12, 24, 384)
    probe = lax.axis_index("probe").astype(jnp.int32).reshape(1)
    col = lax.axis_index("col").astype(jnp.int32).reshape(1)

    def shape(s, t=BF16):
        return jax.ShapeDtypeStruct(s, t)

    def held(s, t=BF16):
        return pltpu.VMEM(s, t)

    def stored(s, t=BF16):
        return pltpu.HBM(s, t)

    any_space = pl.BlockSpec(memory_space=pl.ANY)
    to_y = call(y_pack_kernel, held((8, 2, 336, 128)), [], [far(state), far(advect_y)],
        [
            pltpu.VMEM((5, 12, 24, 384), BF16),
            pltpu.VMEM((12, 24, 384), BF16),
            pltpu.SemaphoreType.DMA((4,)),
        ],
        stay=True,
    )
    at_y = lax.all_to_all(
        to_y.reshape(16, 336, 128), "row", split_axis=0, concat_axis=0, tiled=True
    )
    to_z = call(z_pack_kernel, [stored((648, 128))] + [held((648, 128))] * 7, [col], [state, advect_z])
    at_z = list(to_z)
    for r in ROUTES:
        at_z[r] = shift(to_z[r], r)
    lines_y, lines_z = call(
        matrices_kernel,
        [stored((1152, 384)), stored((384, 192))],
        [col],
        [far(deriv_y), far(deriv_z)],
    )
    term_y = call(y_kernel, stored((16, 336, 128)), [diffusivity], [near(at_y), far(lines_y)])
    back_y = lax.all_to_all(term_y, "row", split_axis=0, concat_axis=0, tiled=True)
    term_z = call(
        z_kernel,
        [stored((552, 128))] + [held((552, 128))] * 7,
        [diffusivity],
        [far(at_z[0])] + [near(x) for x in at_z[1:]] + [far(lines_z)],
    )
    back_z = list(term_z)
    for r in ROUTES:
        back_z[r] = shift(term_z[r], -r)
    base = call(
        xy_kernel,
        held((5, 12, 24, 384), F32),
        [diffusivity],
        [state, forced, advect_x, deriv_x, near(back_y.reshape(8, 2, 336, 128))],
        [pltpu.VMEM((24, 24, 384), F32)],
    )
    pieces = [far(back_z[0])] + [near(x) for x in back_z[1:]]
    sections, sketches, halves = [], [], []
    for p in range(3):
        count = 2 if p < 2 else 1
        section, send, own = call(
            functools.partial(join_kernel, p),
            [shape((5, 12, 24, 384)), held((tiles_of(p), 24, 128)), held((tiles_of(p), 24, 128))],
            [probe, col],
            [near(base)] + pieces,
            [
                pltpu.VMEM((count, 12, 24, 384), BF16),
                pltpu.SemaphoreType.DMA((count,)),
            ],
            kept=sections[-1:],
            spaces=[any_space, vspec(), vspec()],
        )
        sections.append(section)
        halves.append((own, lax.ppermute(send, "probe", [(0, 1), (1, 0)])))
    for p in range(3):
        count = 2 if p < 2 else 1
        own, recv = halves[p]
        sketches.append(
            call(
                functools.partial(sketch_kernel, p),
                [shape((2, 5, 12, 24, 192))],
                [probe, test_mix],
                [near(own), near(recv)],
                [pltpu.VMEM((count, 2, 12, 24, 192), BF16), pltpu.SemaphoreType.DMA((count, 2))],
                kept=sketches[-1:],
                spaces=[any_space],
            )[0]
        )
    section, sketch = sections[-1], sketches[-1]
    return (section[None], sketch)


def solution(mesh):
    placed = (
        P("probe", None, "row", "col", None),
        P("probe", None, "row", "col", None),
        P("row", "col", None),
        P("row", "col", None),
        P("row", "col", None),
        P(),
        P(),
        P(),
        P(),
        P(),
    )

    return jax.shard_map(
        on_device,
        mesh=mesh,
        in_specs=placed,
        out_specs=(P("probe", None, "row", "col", None), P(None, None, "row", "col", "probe")),
        check_vma=False,
    )
```

```python
import functools

import jax
import jax.numpy as jnp
from jax import lax
from jax.experimental import pallas as pl
from jax.experimental.pallas import tpu as pltpu
from jax.sharding import PartitionSpec as P


step_size = 0.25


F32 = jnp.float32
BF16 = jnp.bfloat16


def vspec():
    return pl.BlockSpec(memory_space=pltpu.VMEM)


def sspec():
    return pl.BlockSpec(memory_space=pltpu.SMEM)


def swap(x):
    return pltpu.roll(x, 64, x.ndim - 1)


def low_lanes(shape):
    return lax.broadcasted_iota(jnp.int32, shape, len(shape) - 1) < 64


def merge(half, first, second):
    low = low_lanes(first.shape)
    if half == 0:
        return jnp.where(low, first, swap(second))
    return jnp.where(low, swap(first), second)


def z_pack_kernel(col, state, adv, *outs):
    me = col[0]
    for r in range(8):
        dest = lax.rem(me + r, 8)
        a = dest // 2

        def fill(b, r=r, a=a):
            def body(yl, carry):
                y = 3 * a + yl
                base = pl.multiple_of(yl * 216, 8)
                full = slice(256 * b, 256 * b + 128)
                for u in range(6):
                    src = state[u, y, :, full] if u < 5 else adv[y, :, full]
                    outs[r][pl.ds(base + 24 * u, 24), :] = src
                mid = [state[u, y, :, 128:256].astype(F32) for u in range(5)]
                mid.append(adv[y, :, 128:256].astype(F32))
                for q in range(3):
                    tile = merge(b, mid[2 * q], mid[2 * q + 1])
                    outs[r][pl.ds(base + 144 + 24 * q, 24), :] = tile.astype(BF16)
                return carry

            lax.fori_loop(0, 3, body, 0)

        @pl.when(lax.rem(dest, 2) == 0)
        def _():
            fill(0)

        @pl.when(lax.rem(dest, 2) == 1)
        def _():
            fill(1)


def y_pack_kernel(state_far, adv_far, out, state, adv, sem):
    copies = [
        pltpu.make_async_copy(state_far.at[0:2], state.at[0:2], sem.at[0]),
        pltpu.make_async_copy(state_far.at[2:4], state.at[2:4], sem.at[1]),
        pltpu.make_async_copy(state_far.at[4], state.at[4], sem.at[2]),
        pltpu.make_async_copy(adv_far, adv, sem.at[3]),
    ]
    for copy in copies:
        copy.start()

    def lines(p, c):
        lanes = slice(128 * c, 128 * c + 128)
        if p < 2:
            block = state[2 * p : 2 * p + 2, :, :, lanes].astype(F32).reshape(24, 24, 128)
        else:
            block = jnp.concatenate([state[4, :, :, lanes], adv[:, :, lanes]], axis=0).astype(F32)
        return jnp.swapaxes(block, 0, 1)

    for p in range(3):
        for copy in copies[p : p + 1 if p < 2 else 4]:
            copy.wait()
        for b in range(2):
            out[:, b, 72 * p : 72 * p + 72, :] = lines(p, 2 * b).reshape(8, 72, 128).astype(BF16)
    mid = [lines(p, 1) for p in range(2)]
    for b in range(2):
        tile = merge(b, mid[0], mid[1])
        out[:, b, 216:288, :] = tile.reshape(8, 72, 128).astype(BF16)
    last = lines(2, 1).reshape(8, 3, 24, 128)
    none = jnp.zeros((8, 24, 128), F32)
    for b in range(2):
        out[:, b, 288:312, :] = merge(b, last[:, 0], last[:, 1]).astype(BF16)
        out[:, b, 312:336, :] = merge(b, last[:, 2], none).astype(BF16)


def xy_kernel(coef, state, forcing, adv, mat, back_y, out, work):
    lhs_mat = mat[...].reshape(768, 384)
    low3 = low_lanes((24, 24, 128))
    low8 = low_lanes((8, 24, 128))

    def put_lines(c, block):
        work[:, :, 128 * c : 128 * c + 128] = jnp.swapaxes(block, 0, 1)

    def y_tile(b, at, n):
        return back_y[:, b, at : at + 24 * n, :].astype(F32)

    for p in range(3):
        for b in range(2):
            put_lines(2 * b, y_tile(b, 72 * p, 3).reshape(24, 24, 128))
        if p < 2:
            m = [y_tile(b, 216, 3).reshape(24, 24, 128) for b in range(2)]
            if p == 0:
                put_lines(1, jnp.where(low3, m[0], swap(m[1])))
            else:
                put_lines(1, jnp.where(low3, swap(m[0]), m[1]))
        else:
            m = [[y_tile(b, 288 + 24 * j, 1) for j in range(2)] for b in range(2)]
            parts = [
                jnp.where(low8, m[0][0], swap(m[1][0])),
                jnp.where(low8, swap(m[0][0]), m[1][0]),
                jnp.where(low8, m[0][1], swap(m[1][1])),
            ]
            put_lines(1, jnp.stack(parts, axis=1).reshape(24, 24, 128))
        for i in range(2 if p < 2 else 1):
            v = 2 * p + i
            for h in range(2):
                ys = slice(6 * h, 6 * h + 6)
                field = state[v, ys].astype(F32).reshape(144, 384)
                grad = lax.dot_general(
                    field.astype(BF16),
                    lhs_mat,
                    (((1,), (1,)), ((), ())),
                    preferred_element_type=F32,
                )
                vel = adv[ys].astype(F32).reshape(144, 384)
                frc = forcing[v, ys].astype(F32).reshape(144, 384)
                term = coef[v] * grad[:, 384:] - vel * grad[:, :384]
                term = term + work[12 * i + 6 * h : 12 * i + 6 * h + 6].reshape(144, 384)
                out[v, ys] = (field + step_size * (term + frc)).reshape(6, 24, 384)


def matrices_kernel(col, mat_y, mat_z, lines_y, lines_z):
    me = col[0]
    point = lax.broadcasted_iota(jnp.int32, (192, 192), 0)
    place = lax.broadcasted_iota(jnp.int32, (192, 192), 1)
    block = jnp.zeros((192, 192), jnp.int32)
    for r in range(8):
        inside = (place >= 24 * r) & (place < 24 * r + 24)
        block = jnp.where(inside, 24 * lax.rem(me - r + 8, 8) - 24 * r, block)
    order = jnp.where(point == place + block, 1.0, 0.0).astype(BF16)
    for k in range(2):
        cols = jnp.dot(mat_z[k], order, preferred_element_type=F32).astype(BF16)
        rows = lax.dot_general(order, cols, (((0,), (0,)), ((), ())), preferred_element_type=F32)
        lines_z[192 * k : 192 * k + 192, :] = rows.astype(BF16)

    def spots(index):
        q = lax.shift_right_logical(index * 5462, 16)
        return lax.rem(q, 2), 12 * lax.shift_right_logical(q, 1) + index - 12 * q

    member, line = spots(lax.broadcasted_iota(jnp.int32, (384, 192), 0))
    same = line == lax.broadcasted_iota(jnp.int32, (384, 192), 1)
    spread = [jnp.where(same & (member == m), 1.0, 0.0).astype(BF16) for m in range(2)]
    for k in range(2):
        acc = jnp.zeros((384, 384), F32)
        for m in range(2):
            left = jnp.dot(spread[m], mat_y[k], preferred_element_type=F32).astype(BF16)
            acc = acc + lax.dot_general(
                left, spread[m], (((1,), (1,)), ((), ())), preferred_element_type=F32
            )
        lines_y[384 * k : 384 * k + 384, :] = acc.astype(BF16)
    line_to = spots(lax.broadcasted_iota(jnp.int32, (384, 384), 0))[1]
    member_from, line_from = spots(lax.broadcasted_iota(jnp.int32, (384, 384), 1))
    pick = (line_to == line_from) & (member_from == 1)
    lines_y[768:1152, :] = jnp.where(pick, 1.0, 0.0).astype(BF16)


def z_kernel(coef, *refs):
    recv, lines, outs = refs[:8], refs[8], refs[9:]
    low = low_lanes((192, 128))
    lhs = lines[...]

    def tile(yl, t):
        at = yl * 216 + 24 * t
        return jnp.concatenate([ref[at : at + 24, :].astype(F32) for ref in recv], axis=0)

    def put(t, term):
        for r in range(8):
            outs[r][24 * t : 24 * t + 24, :] = term[24 * r : 24 * r + 24].astype(BF16)

    tails = []
    for yl in range(3):
        tiles = [tile(yl, t) for t in range(9)]
        vel = tiles[5]
        vel_half = jnp.where(low, swap(tiles[8]), tiles[8])
        names = [0, 1, 2, 3, 4, 6, 7, 8]
        for n in range(0, 8, 2):
            rhs = jnp.concatenate([tiles[names[n]], tiles[names[n + 1]]], axis=1).astype(BF16)
            grad = jnp.dot(lhs, rhs, preferred_element_type=F32)
            for j in range(2):
                t = names[n + j]
                g0 = grad[:192, 128 * j : 128 * j + 128]
                g1 = grad[192:, 128 * j : 128 * j + 128]
                if t < 5:
                    put(yl * 7 + t, coef[t] * g1 - vel * g0)
                elif t < 8:
                    q = t - 6
                    c = jnp.where(low, coef[2 * q], coef[2 * q + 1])
                    put(yl * 7 + 5 + q, c * g1 - vel_half * g0)
                else:
                    tails.append(coef[4] * g1 - vel_half * g0)
    put(21, jnp.where(low, tails[0], swap(tails[1])))
    put(22, jnp.where(low, tails[2], 0.0))


def y_kernel(coef, recv, lines, out):
    lhs = lines[0:768, :]
    take = lines[768:1152, :]
    low = low_lanes((384, 128))
    member = lax.broadcasted_iota(jnp.int32, (16, 24, 128), 1).reshape(384, 128) >= 12

    def tile(t):
        return recv[:, 24 * t : 24 * t + 24, :].astype(F32).reshape(384, 128).astype(BF16)

    def put(t, term):
        out[:, 24 * t : 24 * t + 24, :] = term.reshape(16, 24, 128).astype(BF16)

    def coef_of(p):
        if p == 2:
            return jnp.where(member, 0.0, coef[4])
        return jnp.where(member, coef[2 * p + 1], coef[2 * p])

    vel_tail = jnp.dot(
        take, jnp.concatenate([tile(12), tile(13)], axis=1), preferred_element_type=F32
    )
    tail = [vel_tail[:, :128], vel_tail[:, 128:]]
    vel_half = [
        jnp.where(low, tail[0], swap(tail[0])),
        jnp.where(low, swap(tail[0]), tail[0]),
        jnp.where(low, tail[1], swap(tail[1])),
    ]

    work = [(12, tail[0], coef_of(2)), (13, tail[1], coef_of(2))]
    vel_full = jnp.dot(
        take, jnp.concatenate([tile(6), tile(7)], axis=1), preferred_element_type=F32
    )
    vels = [vel_full[:, :128], vel_full[:, 128:]]
    vels.append(jnp.dot(take, tile(8), preferred_element_type=F32))
    for zl in range(3):
        work += [(3 * p + zl, vels[zl], coef_of(p)) for p in range(3)]
        work.append((9 + zl, vel_half[zl], jnp.where(low, coef_of(0), coef_of(1))))
    for n in range(0, 14, 2):
        pair = work[n : n + 2]
        rhs = jnp.concatenate([tile(t) for t, _, _ in pair], axis=1)
        grad = jnp.dot(lhs, rhs, preferred_element_type=F32)
        for k, (t, vel, c) in enumerate(pair):
            lanes = slice(128 * k, 128 * k + 128)
            put(t, c * grad[384:, lanes] - vel * grad[:384, lanes])


CHUNKS = (((4, 5), (3, 4)), ((2, 3), (5, 6)), ((0, 1), (1, 2)), ((6, 7), (7, 0)))


def needs(n):
    return sorted(set(CHUNKS[n][0] + CHUNKS[n][1]))


def group_of(n, me):
    even, odd = CHUNKS[n]
    return lax.rem(me + jnp.where(lax.rem(me, 2) == 0, even[0], odd[0]), 8) // 2


def join_kernel(n, probe, col, *refs):
    base, arrivals = refs[0], dict(zip(needs(n), refs[1:]))
    out, send, own, rows, sem = refs[-5:]
    first = probe[0] == 0
    me = col[0]
    low = low_lanes((24, 128))
    group = group_of(n, me)

    def give(t, half0, half1):
        send[t] = jnp.where(first, half1, half0).astype(BF16)
        own[t] = jnp.where(first, half0, half1).astype(BF16)

    def fill(pair):
        def z_tile(b, t):
            return arrivals[pair[b]][24 * t : 24 * t + 24, :].astype(F32)

        tails = []
        for yl in range(3):
            y = 3 * group + yl
            mids = []
            for v in range(5):
                full = [z_tile(b, 7 * yl + v) for b in range(2)]
                t, odd = (7 * yl + 5 + v // 2, v % 2) if v < 4 else (21 + yl // 2, yl % 2)
                m = [z_tile(b, t) for b in range(2)]
                if odd:
                    mid = jnp.where(low, swap(m[0]), m[1])
                else:
                    mid = jnp.where(low, m[0], swap(m[1]))
                res = []
                for c, part in enumerate((full[0], mid, full[1])):
                    lanes = slice(128 * c, 128 * c + 128)
                    total = (base[v, y, :, lanes] + step_size * part).astype(BF16)
                    rows[v, yl, :, lanes] = total
                    res.append(total.astype(F32))
                give(5 * yl + v, res[0], res[2])
                mids.append(res[1])
            for q in range(2):
                two = mids[2 * q : 2 * q + 2]
                give(15 + 2 * yl + q, merge(0, *two), merge(1, *two))
            tails.append(mids[4])
        tails.append(jnp.zeros((24, 128), F32))
        for q in range(2):
            two = tails[2 * q : 2 * q + 2]
            give(21 + q, merge(0, *two), merge(1, *two))

    for odd_me in range(2):

        @pl.when(lax.rem(me, 2) == odd_me)
        def _(odd_me=odd_me):
            fill(CHUNKS[n][odd_me])

    copy = pltpu.make_async_copy(rows, out.at[:, pl.ds(3 * group, 3)], sem)
    copy.start()
    copy.wait()


def sketch_kernel(n, probe, col, mix, *refs):
    own, recv = refs[:2]
    out, rows, sem = refs[-3:]
    p = probe[0]
    low = low_lanes((24, 128))
    group = group_of(n, col[0])

    def mixed(t, g):
        a = (own[t].astype(F32) * mix[p, g]).astype(BF16).astype(F32)
        b = (recv[t].astype(F32) * mix[1 - p, g]).astype(BF16).astype(F32)
        return a + b

    def put(g, v, yl, full, piece):
        turned = swap(full)
        head = jnp.where(p == 0, full, jnp.where(low, piece, turned))
        tail = jnp.where(p == 0, piece, turned)
        rows[g, v, yl, :, 0:128] = head.astype(BF16)
        rows[g, v, yl, :, 128:192] = tail[:, :64].astype(BF16)

    for g in range(2):
        for yl in range(3):
            for q in range(2):
                half = mixed(15 + 2 * yl + q, g)
                put(g, 2 * q, yl, mixed(5 * yl + 2 * q, g), half)
                put(g, 2 * q + 1, yl, mixed(5 * yl + 2 * q + 1, g), swap(half))
        half = mixed(21, g)
        put(g, 4, 0, mixed(4, g), half)
        put(g, 4, 1, mixed(9, g), swap(half))
        put(g, 4, 2, mixed(14, g), mixed(22, g))
    copy = pltpu.make_async_copy(rows, out.at[:, :, pl.ds(3 * group, 3)], sem)
    copy.start()
    copy.wait()


def call(kernel, out_shapes, scalars, arrays, scratch=(), kept=(), spaces=None, stay=False):
    many = isinstance(out_shapes, (list, tuple))
    specs = spaces or [vspec() for _ in (out_shapes if many else [0])]
    before = len(scalars) + len(arrays)
    return pl.pallas_call(
        kernel,
        out_shape=out_shapes,
        in_specs=[sspec()] * len(scalars)
        + [pl.BlockSpec(memory_space=pl.ANY) if stay else vspec()] * len(arrays)
        + [pl.BlockSpec(memory_space=pl.ANY)] * len(kept),
        out_specs=specs if many else specs[0],
        scratch_shapes=scratch,
        input_output_aliases={before + n: n for n in range(len(kept))},
        compiler_params=pltpu.CompilerParams(vmem_limit_bytes=16 << 20),
    )(*scalars, *arrays, *kept)


def far(x):
    return pltpu.with_memory_space_constraint(x, pltpu.HBM)


def near(x):
    return pltpu.with_memory_space_constraint(x, pltpu.VMEM)


def shift(x, distance):
    return lax.ppermute(x, "col", [(i, (i + distance) % 8) for i in range(8)])


ROUTES = (3, 5, 4, 2, 6, 1, 7)


def on_device(
    flow_state,
    forcing,
    advect_x,
    advect_y,
    advect_z,
    diffusivity,
    deriv_x,
    deriv_y,
    deriv_z,
    test_mix,
):
    state = flow_state.reshape(5, 12, 24, 384)
    forced = forcing.reshape(5, 12, 24, 384)
    probe = lax.axis_index("probe").astype(jnp.int32).reshape(1)
    col = lax.axis_index("col").astype(jnp.int32).reshape(1)

    def shape(s, t=BF16):
        return jax.ShapeDtypeStruct(s, t)

    def held(s, t=BF16):
        return pltpu.VMEM(s, t)

    def stored(s, t=BF16):
        return pltpu.HBM(s, t)

    any_space = pl.BlockSpec(memory_space=pl.ANY)
    to_y = call(y_pack_kernel, held((8, 2, 336, 128)), [], [far(state), far(advect_y)],
        [
            pltpu.VMEM((5, 12, 24, 384), BF16),
            pltpu.VMEM((12, 24, 384), BF16),
            pltpu.SemaphoreType.DMA((4,)),
        ],
        stay=True,
    )
    at_y = lax.all_to_all(
        to_y.reshape(16, 336, 128), "row", split_axis=0, concat_axis=0, tiled=True
    )
    to_z = call(z_pack_kernel, [stored((648, 128))] + [held((648, 128))] * 7, [col], [state, advect_z])
    at_z = list(to_z)
    for r in ROUTES:
        at_z[r] = shift(to_z[r], r)
    lines_y, lines_z = call(
        matrices_kernel,
        [stored((1152, 384)), stored((384, 192))],
        [col],
        [far(deriv_y), far(deriv_z)],
    )
    term_y = call(y_kernel, stored((16, 336, 128)), [diffusivity], [near(at_y), far(lines_y)])
    back_y = lax.all_to_all(term_y, "row", split_axis=0, concat_axis=0, tiled=True)
    term_z = call(
        z_kernel,
        [stored((552, 128))] + [held((552, 128))] * 7,
        [diffusivity],
        [far(at_z[0])] + [near(x) for x in at_z[1:]] + [far(lines_z)],
    )
    back_z = list(term_z)
    for r in ROUTES:
        back_z[r] = shift(term_z[r], -r)
    base = call(
        xy_kernel,
        held((5, 12, 24, 384), F32),
        [diffusivity],
        [state, forced, advect_x, deriv_x, near(back_y.reshape(8, 2, 336, 128))],
        [pltpu.VMEM((24, 24, 384), F32)],
    )
    pieces = [far(back_z[0])] + [near(x) for x in back_z[1:]]
    sections, sketches, halves = [], [], []
    for n in range(4):
        section, send, own = call(
            functools.partial(join_kernel, n),
            [shape((5, 12, 24, 384)), held((23, 24, 128)), held((23, 24, 128))],
            [probe, col],
            [near(base)] + [pieces[r] for r in needs(n)],
            [pltpu.VMEM((5, 3, 24, 384), BF16), pltpu.SemaphoreType.DMA],
            kept=sections[-1:],
            spaces=[any_space, vspec(), vspec()],
        )
        sections.append(section)
        halves.append((own, lax.ppermute(send, "probe", [(0, 1), (1, 0)])))
    for n in range(4):
        own, recv = halves[n]
        sketches.append(
            call(
                functools.partial(sketch_kernel, n),
                [shape((2, 5, 12, 24, 192))],
                [probe, col, test_mix],
                [near(own), near(recv)],
                [pltpu.VMEM((2, 5, 3, 24, 192), BF16), pltpu.SemaphoreType.DMA],
                kept=sketches[-1:],
                spaces=[any_space],
            )[0]
        )
    section, sketch = sections[-1], sketches[-1]
    return (section[None], sketch)


def solution(mesh):
    placed = (
        P("probe", None, "row", "col", None),
        P("probe", None, "row", "col", None),
        P("row", "col", None),
        P("row", "col", None),
        P("row", "col", None),
        P(),
        P(),
        P(),
        P(),
        P(),
    )

    return jax.shard_map(
        on_device,
        mesh=mesh,
        in_specs=placed,
        out_specs=(P("probe", None, "row", "col", None), P(None, None, "row", "col", "probe")),
        check_vma=False,
    )
```

```python
import functools

import jax
import jax.numpy as jnp
from jax import lax
from jax.experimental import pallas as pl
from jax.experimental.pallas import tpu as pltpu
from jax.sharding import PartitionSpec as P


step_size = 0.25


F32 = jnp.float32
BF16 = jnp.bfloat16


def vspec():
    return pl.BlockSpec(memory_space=pltpu.VMEM)


def sspec():
    return pl.BlockSpec(memory_space=pltpu.SMEM)


def swap(x):
    return pltpu.roll(x, 64, x.ndim - 1)


def low_lanes(shape):
    return lax.broadcasted_iota(jnp.int32, shape, len(shape) - 1) < 64


def merge(half, first, second):
    low = low_lanes(first.shape)
    if half == 0:
        return jnp.where(low, first, swap(second))
    return jnp.where(low, swap(first), second)


def z_pack_kernel(distances, col, state, adv, *outs):
    me = col[0]
    outs = dict(zip(distances, outs))
    for r in distances:
        dest = lax.rem(me + r, 8)
        a = dest // 2

        def fill(b, r=r, a=a):
            def body(yl, carry):
                y = 3 * a + yl
                base = pl.multiple_of(yl * 216, 8)
                full = slice(256 * b, 256 * b + 128)
                for u in range(6):
                    src = state[u, y, :, full] if u < 5 else adv[y, :, full]
                    outs[r][pl.ds(base + 24 * u, 24), :] = src
                mid = [state[u, y, :, 128:256].astype(F32) for u in range(5)]
                mid.append(adv[y, :, 128:256].astype(F32))
                for q in range(3):
                    tile = merge(b, mid[2 * q], mid[2 * q + 1])
                    outs[r][pl.ds(base + 144 + 24 * q, 24), :] = tile.astype(BF16)
                return carry

            lax.fori_loop(0, 3, body, 0)

        @pl.when(lax.rem(dest, 2) == 0)
        def _():
            fill(0)

        @pl.when(lax.rem(dest, 2) == 1)
        def _():
            fill(1)


def y_pack_kernel(state_far, adv_far, out, state, adv, sem):
    copies = [
        pltpu.make_async_copy(state_far.at[0:2], state.at[0:2], sem.at[0]),
        pltpu.make_async_copy(state_far.at[2:4], state.at[2:4], sem.at[1]),
        pltpu.make_async_copy(state_far.at[4], state.at[4], sem.at[2]),
        pltpu.make_async_copy(adv_far, adv, sem.at[3]),
    ]
    for copy in copies:
        copy.start()

    def lines(p, c):
        lanes = slice(128 * c, 128 * c + 128)
        if p < 2:
            block = state[2 * p : 2 * p + 2, :, :, lanes].astype(F32).reshape(24, 24, 128)
        else:
            block = jnp.concatenate([state[4, :, :, lanes], adv[:, :, lanes]], axis=0).astype(F32)
        return jnp.swapaxes(block, 0, 1)

    for p in range(3):
        for copy in copies[p : p + 1 if p < 2 else 4]:
            copy.wait()
        for b in range(2):
            out[:, b, 72 * p : 72 * p + 72, :] = lines(p, 2 * b).reshape(8, 72, 128).astype(BF16)
    mid = [lines(p, 1) for p in range(2)]
    for b in range(2):
        tile = merge(b, mid[0], mid[1])
        out[:, b, 216:288, :] = tile.reshape(8, 72, 128).astype(BF16)
    last = lines(2, 1).reshape(8, 3, 24, 128)
    none = jnp.zeros((8, 24, 128), F32)
    for b in range(2):
        out[:, b, 288:312, :] = merge(b, last[:, 0], last[:, 1]).astype(BF16)
        out[:, b, 312:336, :] = merge(b, last[:, 2], none).astype(BF16)


def xy_kernel(coef, state, forcing, adv, mat, back_y, out, work):
    lhs_mat = mat[...].reshape(768, 384)
    low3 = low_lanes((24, 24, 128))
    low8 = low_lanes((8, 24, 128))

    def put_lines(c, block):
        work[:, :, 128 * c : 128 * c + 128] = jnp.swapaxes(block, 0, 1)

    def y_tile(b, at, n):
        return back_y[:, b, at : at + 24 * n, :].astype(F32)

    for p in range(3):
        for b in range(2):
            put_lines(2 * b, y_tile(b, 72 * p, 3).reshape(24, 24, 128))
        if p < 2:
            m = [y_tile(b, 216, 3).reshape(24, 24, 128) for b in range(2)]
            if p == 0:
                put_lines(1, jnp.where(low3, m[0], swap(m[1])))
            else:
                put_lines(1, jnp.where(low3, swap(m[0]), m[1]))
        else:
            m = [[y_tile(b, 288 + 24 * j, 1) for j in range(2)] for b in range(2)]
            parts = [
                jnp.where(low8, m[0][0], swap(m[1][0])),
                jnp.where(low8, swap(m[0][0]), m[1][0]),
                jnp.where(low8, m[0][1], swap(m[1][1])),
            ]
            put_lines(1, jnp.stack(parts, axis=1).reshape(24, 24, 128))
        for i in range(2 if p < 2 else 1):
            v = 2 * p + i
            for h in range(2):
                ys = slice(6 * h, 6 * h + 6)
                field = state[v, ys].astype(F32).reshape(144, 384)
                grad = lax.dot_general(
                    field.astype(BF16),
                    lhs_mat,
                    (((1,), (1,)), ((), ())),
                    preferred_element_type=F32,
                )
                vel = adv[ys].astype(F32).reshape(144, 384)
                frc = forcing[v, ys].astype(F32).reshape(144, 384)
                term = coef[v] * grad[:, 384:] - vel * grad[:, :384]
                term = term + work[12 * i + 6 * h : 12 * i + 6 * h + 6].reshape(144, 384)
                out[v, ys] = (field + step_size * (term + frc)).reshape(6, 24, 384)


def matrices_kernel(col, mat_y, mat_z, lines_y, lines_z):
    me = col[0]
    point = lax.broadcasted_iota(jnp.int32, (192, 192), 0)
    place = lax.broadcasted_iota(jnp.int32, (192, 192), 1)
    block = jnp.zeros((192, 192), jnp.int32)
    for r in range(8):
        inside = (place >= 24 * r) & (place < 24 * r + 24)
        block = jnp.where(inside, 24 * lax.rem(me - r + 8, 8) - 24 * r, block)
    order = jnp.where(point == place + block, 1.0, 0.0).astype(BF16)
    for k in range(2):
        cols = jnp.dot(mat_z[k], order, preferred_element_type=F32).astype(BF16)
        rows = lax.dot_general(order, cols, (((0,), (0,)), ((), ())), preferred_element_type=F32)
        lines_z[192 * k : 192 * k + 192, :] = rows.astype(BF16)

    def spots(index):
        q = lax.shift_right_logical(index * 5462, 16)
        return lax.rem(q, 2), 12 * lax.shift_right_logical(q, 1) + index - 12 * q

    member, line = spots(lax.broadcasted_iota(jnp.int32, (384, 192), 0))
    same = line == lax.broadcasted_iota(jnp.int32, (384, 192), 1)
    spread = [jnp.where(same & (member == m), 1.0, 0.0).astype(BF16) for m in range(2)]
    for k in range(2):
        acc = jnp.zeros((384, 384), F32)
        for m in range(2):
            left = jnp.dot(spread[m], mat_y[k], preferred_element_type=F32).astype(BF16)
            acc = acc + lax.dot_general(
                left, spread[m], (((1,), (1,)), ((), ())), preferred_element_type=F32
            )
        lines_y[384 * k : 384 * k + 384, :] = acc.astype(BF16)
    line_to = spots(lax.broadcasted_iota(jnp.int32, (384, 384), 0))[1]
    member_from, line_from = spots(lax.broadcasted_iota(jnp.int32, (384, 384), 1))
    pick = (line_to == line_from) & (member_from == 1)
    lines_y[768:1152, :] = jnp.where(pick, 1.0, 0.0).astype(BF16)


def z_kernel(coef, *refs):
    recv, lines, outs = refs[:8], refs[8], refs[9:]
    low = low_lanes((192, 128))
    lhs = lines[...]

    def tile(yl, t):
        at = yl * 216 + 24 * t
        return jnp.concatenate([ref[at : at + 24, :].astype(F32) for ref in recv], axis=0)

    def put(t, term):
        for r in range(8):
            outs[r][24 * t : 24 * t + 24, :] = term[24 * r : 24 * r + 24].astype(BF16)

    tails = []
    for yl in range(3):
        tiles = [tile(yl, t) for t in range(9)]
        vel = tiles[5]
        vel_half = jnp.where(low, swap(tiles[8]), tiles[8])
        names = [0, 1, 2, 3, 4, 6, 7, 8]
        for n in range(0, 8, 2):
            rhs = jnp.concatenate([tiles[names[n]], tiles[names[n + 1]]], axis=1).astype(BF16)
            grad = jnp.dot(lhs, rhs, preferred_element_type=F32)
            for j in range(2):
                t = names[n + j]
                g0 = grad[:192, 128 * j : 128 * j + 128]
                g1 = grad[192:, 128 * j : 128 * j + 128]
                if t < 5:
                    put(yl * 7 + t, coef[t] * g1 - vel * g0)
                elif t < 8:
                    q = t - 6
                    c = jnp.where(low, coef[2 * q], coef[2 * q + 1])
                    put(yl * 7 + 5 + q, c * g1 - vel_half * g0)
                else:
                    tails.append(coef[4] * g1 - vel_half * g0)
    put(21, jnp.where(low, tails[0], swap(tails[1])))
    put(22, jnp.where(low, tails[2], 0.0))


def y_kernel(coef, recv, lines, out):
    lhs = lines[0:768, :]
    take = lines[768:1152, :]
    low = low_lanes((384, 128))
    member = lax.broadcasted_iota(jnp.int32, (16, 24, 128), 1).reshape(384, 128) >= 12

    def tile(t):
        return recv[:, 24 * t : 24 * t + 24, :].astype(F32).reshape(384, 128).astype(BF16)

    def put(t, term):
        out[:, 24 * t : 24 * t + 24, :] = term.reshape(16, 24, 128).astype(BF16)

    def coef_of(p):
        if p == 2:
            return jnp.where(member, 0.0, coef[4])
        return jnp.where(member, coef[2 * p + 1], coef[2 * p])

    vel_tail = jnp.dot(
        take, jnp.concatenate([tile(12), tile(13)], axis=1), preferred_element_type=F32
    )
    tail = [vel_tail[:, :128], vel_tail[:, 128:]]
    vel_half = [
        jnp.where(low, tail[0], swap(tail[0])),
        jnp.where(low, swap(tail[0]), tail[0]),
        jnp.where(low, tail[1], swap(tail[1])),
    ]

    work = [(12, tail[0], coef_of(2)), (13, tail[1], coef_of(2))]
    vel_full = jnp.dot(
        take, jnp.concatenate([tile(6), tile(7)], axis=1), preferred_element_type=F32
    )
    vels = [vel_full[:, :128], vel_full[:, 128:]]
    vels.append(jnp.dot(take, tile(8), preferred_element_type=F32))
    for zl in range(3):
        work += [(3 * p + zl, vels[zl], coef_of(p)) for p in range(3)]
        work.append((9 + zl, vel_half[zl], jnp.where(low, coef_of(0), coef_of(1))))
    for n in range(0, 14, 2):
        pair = work[n : n + 2]
        rhs = jnp.concatenate([tile(t) for t, _, _ in pair], axis=1)
        grad = jnp.dot(lhs, rhs, preferred_element_type=F32)
        for k, (t, vel, c) in enumerate(pair):
            lanes = slice(128 * k, 128 * k + 128)
            put(t, c * grad[384:, lanes] - vel * grad[:384, lanes])


CHUNKS = (((0, 1), (7, 0)), ((4, 5), (3, 4)), ((2, 3), (1, 2)), ((6, 7), (5, 6)))


def needs(n):
    return sorted(set(CHUNKS[n][0] + CHUNKS[n][1]))


def group_of(n, me):
    even, odd = CHUNKS[n]
    return lax.rem(me + jnp.where(lax.rem(me, 2) == 0, even[0], odd[0]), 8) // 2


def join_kernel(n, probe, col, *refs):
    base, arrivals = refs[0], dict(zip(needs(n), refs[1:]))
    out, send, own, rows, sem = refs[-5:]
    first = probe[0] == 0
    me = col[0]
    low = low_lanes((24, 128))
    group = group_of(n, me)

    def give(t, half0, half1):
        send[t] = jnp.where(first, half1, half0).astype(BF16)
        own[t] = jnp.where(first, half0, half1).astype(BF16)

    def copy_of(yl):
        return pltpu.make_async_copy(
            rows.at[:, yl], out.at[:, 3 * group + yl], sem.at[yl]
        )

    def fill(pair):
        def z_tile(b, t):
            return arrivals[pair[b]][24 * t : 24 * t + 24, :].astype(F32)

        tails = []
        for yl in range(3):
            y = 3 * group + yl
            mids = []
            for v in range(5):
                full = [z_tile(b, 7 * yl + v) for b in range(2)]
                t, odd = (7 * yl + 5 + v // 2, v % 2) if v < 4 else (21 + yl // 2, yl % 2)
                m = [z_tile(b, t) for b in range(2)]
                if odd:
                    mid = jnp.where(low, swap(m[0]), m[1])
                else:
                    mid = jnp.where(low, m[0], swap(m[1]))
                res = []
                for c, part in enumerate((full[0], mid, full[1])):
                    lanes = slice(128 * c, 128 * c + 128)
                    total = (base[v, y, :, lanes] + step_size * part).astype(BF16)
                    rows[v, yl, :, lanes] = total
                    res.append(total.astype(F32))
                give(5 * yl + v, res[0], res[2])
                mids.append(res[1])
            for q in range(2):
                two = mids[2 * q : 2 * q + 2]
                give(15 + 2 * yl + q, merge(0, *two), merge(1, *two))
            tails.append(mids[4])
            copy_of(yl).start()
        tails.append(jnp.zeros((24, 128), F32))
        for q in range(2):
            two = tails[2 * q : 2 * q + 2]
            give(21 + q, merge(0, *two), merge(1, *two))

    for odd_me in range(2):

        @pl.when(lax.rem(me, 2) == odd_me)
        def _(odd_me=odd_me):
            fill(CHUNKS[n][odd_me])

    for yl in range(3):
        copy_of(yl).wait()


def sketch_kernel(n, probe, col, mix, *refs):
    own, recv = refs[:2]
    out, rows, sem = refs[-3:]
    p = probe[0]
    low = low_lanes((24, 128))
    group = group_of(n, col[0])

    def copy_of(g):
        return pltpu.make_async_copy(rows.at[g], out.at[g, :, pl.ds(3 * group, 3)], sem.at[g])

    def mixed(t, g):
        a = (own[t].astype(F32) * mix[p, g]).astype(BF16).astype(F32)
        b = (recv[t].astype(F32) * mix[1 - p, g]).astype(BF16).astype(F32)
        return a + b

    def put(g, v, yl, full, piece):
        turned = swap(full)
        head = jnp.where(p == 0, full, jnp.where(low, piece, turned))
        tail = jnp.where(p == 0, piece, turned)
        rows[g, v, yl, :, 0:128] = head.astype(BF16)
        rows[g, v, yl, :, 128:192] = tail[:, :64].astype(BF16)

    for g in range(2):
        for yl in range(3):
            for q in range(2):
                half = mixed(15 + 2 * yl + q, g)
                put(g, 2 * q, yl, mixed(5 * yl + 2 * q, g), half)
                put(g, 2 * q + 1, yl, mixed(5 * yl + 2 * q + 1, g), swap(half))
        half = mixed(21, g)
        put(g, 4, 0, mixed(4, g), half)
        put(g, 4, 1, mixed(9, g), swap(half))
        put(g, 4, 2, mixed(14, g), mixed(22, g))
        copy_of(g).start()
    for g in range(2):
        copy_of(g).wait()


def call(kernel, out_shapes, scalars, arrays, scratch=(), kept=(), spaces=None, stay=False):
    many = isinstance(out_shapes, (list, tuple))
    specs = spaces or [vspec() for _ in (out_shapes if many else [0])]
    before = len(scalars) + len(arrays)
    return pl.pallas_call(
        kernel,
        out_shape=out_shapes,
        in_specs=[sspec()] * len(scalars)
        + [pl.BlockSpec(memory_space=pl.ANY) if stay else vspec()] * len(arrays)
        + [pl.BlockSpec(memory_space=pl.ANY)] * len(kept),
        out_specs=specs if many else specs[0],
        scratch_shapes=scratch,
        input_output_aliases={before + n: n for n in range(len(kept))},
        compiler_params=pltpu.CompilerParams(vmem_limit_bytes=16 << 20),
    )(*scalars, *arrays, *kept)


def far(x):
    return pltpu.with_memory_space_constraint(x, pltpu.HBM)


def near(x):
    return pltpu.with_memory_space_constraint(x, pltpu.VMEM)


def shift(x, distance):
    return lax.ppermute(x, "col", [(i, (i + distance) % 8) for i in range(8)])


ROUTES = (1, 7, 3, 5, 4, 2, 6)


def on_device(
    flow_state,
    forcing,
    advect_x,
    advect_y,
    advect_z,
    diffusivity,
    deriv_x,
    deriv_y,
    deriv_z,
    test_mix,
):
    state = flow_state.reshape(5, 12, 24, 384)
    forced = forcing.reshape(5, 12, 24, 384)
    probe = lax.axis_index("probe").astype(jnp.int32).reshape(1)
    col = lax.axis_index("col").astype(jnp.int32).reshape(1)

    def shape(s, t=BF16):
        return jax.ShapeDtypeStruct(s, t)

    def held(s, t=BF16):
        return pltpu.VMEM(s, t)

    def stored(s, t=BF16):
        return pltpu.HBM(s, t)

    any_space = pl.BlockSpec(memory_space=pl.ANY)
    to_y = call(y_pack_kernel, held((8, 2, 336, 128)), [], [far(state), far(advect_y)],
        [
            pltpu.VMEM((5, 12, 24, 384), BF16),
            pltpu.VMEM((12, 24, 384), BF16),
            pltpu.SemaphoreType.DMA((4,)),
        ],
        stay=True,
    )
    at_y = lax.all_to_all(
        to_y.reshape(16, 336, 128), "row", split_axis=0, concat_axis=0, tiled=True
    )
    at_z = {}
    for distances in ((1, 7), (0, 3, 5, 4, 2, 6)):
        to_z = call(
            functools.partial(z_pack_kernel, distances),
            [(held if r else stored)((648, 128)) for r in distances],
            [col],
            [state, advect_z],
        )
        for r, piece in zip(distances, to_z):
            at_z[r] = shift(piece, r) if r else piece
    at_z = [at_z[r] for r in range(8)]
    lines_y, lines_z = call(
        matrices_kernel,
        [stored((1152, 384)), stored((384, 192))],
        [col],
        [far(deriv_y), far(deriv_z)],
    )
    term_y = call(y_kernel, stored((16, 336, 128)), [diffusivity], [near(at_y), far(lines_y)])
    back_y = lax.all_to_all(term_y, "row", split_axis=0, concat_axis=0, tiled=True)
    term_z = call(
        z_kernel,
        [stored((552, 128))] * 8,
        [diffusivity],
        [far(at_z[0])] + [near(x) for x in at_z[1:]] + [far(lines_z)],
    )
    back_z = list(term_z)
    for r in ROUTES:
        back_z[r] = shift(term_z[r], -r)
    base = call(
        xy_kernel,
        held((5, 12, 24, 384), F32),
        [diffusivity],
        [state, far(forced), far(advect_x), far(deriv_x), near(back_y.reshape(8, 2, 336, 128))],
        [pltpu.VMEM((24, 24, 384), F32)],
    )
    pieces = [far(back_z[0])] + [near(x) for x in back_z[1:]]
    sections, sketches, halves = [], [], []
    for n in range(4):
        section, send, own = call(
            functools.partial(join_kernel, n),
            [shape((5, 12, 24, 384)), held((23, 24, 128)), held((23, 24, 128))],
            [probe, col],
            [near(base)] + [pieces[r] for r in needs(n)],
            [pltpu.VMEM((5, 3, 24, 384), BF16), pltpu.SemaphoreType.DMA((3,))],
            kept=sections[-1:],
            spaces=[any_space, vspec(), vspec()],
        )
        sections.append(section)
        halves.append((own, lax.ppermute(send, "probe", [(0, 1), (1, 0)])))
    for n in range(4):
        own, recv = halves[n]
        sketches.append(
            call(
                functools.partial(sketch_kernel, n),
                [shape((2, 5, 12, 24, 192))],
                [probe, col, test_mix],
                [near(own), near(recv)],
                [pltpu.VMEM((2, 5, 3, 24, 192), BF16), pltpu.SemaphoreType.DMA((2,))],
                kept=sketches[-1:],
                spaces=[any_space],
            )[0]
        )
    section, sketch = sections[-1], sketches[-1]
    return (section[None], sketch)


def solution(mesh):
    placed = (
        P("probe", None, "row", "col", None),
        P("probe", None, "row", "col", None),
        P("row", "col", None),
        P("row", "col", None),
        P("row", "col", None),
        P(),
        P(),
        P(),
        P(),
        P(),
    )

    return jax.shard_map(
        on_device,
        mesh=mesh,
        in_specs=placed,
        out_specs=(P("probe", None, "row", "col", None), P(None, None, "row", "col", "probe")),
        check_vma=False,
    )
```

```python
import functools

import jax
import jax.numpy as jnp
from jax import lax
from jax.experimental import pallas as pl
from jax.experimental.pallas import tpu as pltpu
from jax.sharding import PartitionSpec as P


step_size = 0.25


F32 = jnp.float32
BF16 = jnp.bfloat16


def vspec():
    return pl.BlockSpec(memory_space=pltpu.VMEM)


def sspec():
    return pl.BlockSpec(memory_space=pltpu.SMEM)


def swap(x):
    return pltpu.roll(x, 64, x.ndim - 1)


def low_lanes(shape):
    return lax.broadcasted_iota(jnp.int32, shape, len(shape) - 1) < 64


def merge(half, first, second):
    low = low_lanes(first.shape)
    if half == 0:
        return jnp.where(low, first, swap(second))
    return jnp.where(low, swap(first), second)


def z_pack_kernel(distances, col, state, adv, *refs):
    me = col[0]
    held, sem = refs[-2:]
    copies = []
    for n, r in enumerate(distances):
        dest = lax.rem(me + r, 8)
        a = dest // 2

        def fill(b, n=n, a=a):
            def body(yl, carry):
                y = 3 * a + yl
                base = pl.multiple_of(yl * 216, 8)
                full = slice(256 * b, 256 * b + 128)
                for u in range(6):
                    src = state[u, y, :, full] if u < 5 else adv[y, :, full]
                    held[n, pl.ds(base + 24 * u, 24), :] = src
                mid = [state[u, y, :, 128:256].astype(F32) for u in range(5)]
                mid.append(adv[y, :, 128:256].astype(F32))
                for q in range(3):
                    tile = merge(b, mid[2 * q], mid[2 * q + 1])
                    held[n, pl.ds(base + 144 + 24 * q, 24), :] = tile.astype(BF16)
                return carry

            lax.fori_loop(0, 3, body, 0)

        @pl.when(lax.rem(dest, 2) == 0)
        def _():
            fill(0)

        @pl.when(lax.rem(dest, 2) == 1)
        def _():
            fill(1)

        copies.append(pltpu.make_async_copy(held.at[n], refs[n], sem.at[n]))
        copies[-1].start()
    for copy in copies:
        copy.wait()


def y_pack_kernel(state_far, adv_far, out_far, state, adv, out, sem):
    copies = [
        pltpu.make_async_copy(state_far.at[0:2], state.at[0:2], sem.at[0]),
        pltpu.make_async_copy(state_far.at[2:4], state.at[2:4], sem.at[1]),
        pltpu.make_async_copy(state_far.at[4], state.at[4], sem.at[2]),
        pltpu.make_async_copy(adv_far, adv, sem.at[3]),
    ]
    for copy in copies:
        copy.start()
    leaving = []

    def ship(n, first, last):
        rows = slice(first, last)
        copy = pltpu.make_async_copy(out.at[:, :, rows], out_far.at[:, :, rows], sem.at[4 + n])
        copy.start()
        leaving.append(copy)

    def lines(p, c):
        lanes = slice(128 * c, 128 * c + 128)
        if p < 2:
            block = state[2 * p : 2 * p + 2, :, :, lanes].astype(F32).reshape(24, 24, 128)
        else:
            block = jnp.concatenate([state[4, :, :, lanes], adv[:, :, lanes]], axis=0).astype(F32)
        return jnp.swapaxes(block, 0, 1)

    for p in range(3):
        for copy in copies[p : p + 1 if p < 2 else 4]:
            copy.wait()
        for b in range(2):
            out[:, b, 72 * p : 72 * p + 72, :] = lines(p, 2 * b).reshape(8, 72, 128).astype(BF16)
        ship(p, 72 * p, 72 * p + 72)
    mid = [lines(p, 1) for p in range(2)]
    for b in range(2):
        tile = merge(b, mid[0], mid[1])
        out[:, b, 216:288, :] = tile.reshape(8, 72, 128).astype(BF16)
    last = lines(2, 1).reshape(8, 3, 24, 128)
    none = jnp.zeros((8, 24, 128), F32)
    for b in range(2):
        out[:, b, 288:312, :] = merge(b, last[:, 0], last[:, 1]).astype(BF16)
        out[:, b, 312:336, :] = merge(b, last[:, 2], none).astype(BF16)
    ship(3, 216, 336)
    for copy in leaving:
        copy.wait()


def xy_kernel(coef, state, forcing, adv, mat, back_y, out, work):
    lhs_mat = mat[...].reshape(768, 384)
    low3 = low_lanes((24, 24, 128))
    low8 = low_lanes((8, 24, 128))

    def put_lines(c, block):
        work[:, :, 128 * c : 128 * c + 128] = jnp.swapaxes(block, 0, 1)

    def y_tile(b, at, n):
        return back_y[:, b, at : at + 24 * n, :].astype(F32)

    for p in range(3):
        for b in range(2):
            put_lines(2 * b, y_tile(b, 72 * p, 3).reshape(24, 24, 128))
        if p < 2:
            m = [y_tile(b, 216, 3).reshape(24, 24, 128) for b in range(2)]
            if p == 0:
                put_lines(1, jnp.where(low3, m[0], swap(m[1])))
            else:
                put_lines(1, jnp.where(low3, swap(m[0]), m[1]))
        else:
            m = [[y_tile(b, 288 + 24 * j, 1) for j in range(2)] for b in range(2)]
            parts = [
                jnp.where(low8, m[0][0], swap(m[1][0])),
                jnp.where(low8, swap(m[0][0]), m[1][0]),
                jnp.where(low8, m[0][1], swap(m[1][1])),
            ]
            put_lines(1, jnp.stack(parts, axis=1).reshape(24, 24, 128))
        for i in range(2 if p < 2 else 1):
            v = 2 * p + i
            for h in range(2):
                ys = slice(6 * h, 6 * h + 6)
                field = state[v, ys].astype(F32).reshape(144, 384)
                grad = lax.dot_general(
                    field.astype(BF16),
                    lhs_mat,
                    (((1,), (1,)), ((), ())),
                    preferred_element_type=F32,
                )
                vel = adv[ys].astype(F32).reshape(144, 384)
                frc = forcing[v, ys].astype(F32).reshape(144, 384)
                term = coef[v] * grad[:, 384:] - vel * grad[:, :384]
                term = term + work[12 * i + 6 * h : 12 * i + 6 * h + 6].reshape(144, 384)
                out[v, ys] = (field + step_size * (term + frc)).reshape(6, 24, 384)


def matrices_kernel(col, mat_y, mat_z, lines_y, lines_z):
    me = col[0]
    point = lax.broadcasted_iota(jnp.int32, (192, 192), 0)
    place = lax.broadcasted_iota(jnp.int32, (192, 192), 1)
    block = jnp.zeros((192, 192), jnp.int32)
    for r in range(8):
        inside = (place >= 24 * r) & (place < 24 * r + 24)
        block = jnp.where(inside, 24 * lax.rem(me - r + 8, 8) - 24 * r, block)
    order = jnp.where(point == place + block, 1.0, 0.0).astype(BF16)
    for k in range(2):
        cols = jnp.dot(mat_z[k], order, preferred_element_type=F32).astype(BF16)
        rows = lax.dot_general(order, cols, (((0,), (0,)), ((), ())), preferred_element_type=F32)
        lines_z[192 * k : 192 * k + 192, :] = rows.astype(BF16)

    def spots(index):
        q = lax.shift_right_logical(index * 5462, 16)
        return lax.rem(q, 2), 12 * lax.shift_right_logical(q, 1) + index - 12 * q

    member, line = spots(lax.broadcasted_iota(jnp.int32, (384, 192), 0))
    same = line == lax.broadcasted_iota(jnp.int32, (384, 192), 1)
    spread = [jnp.where(same & (member == m), 1.0, 0.0).astype(BF16) for m in range(2)]
    for k in range(2):
        acc = jnp.zeros((384, 384), F32)
        for m in range(2):
            left = jnp.dot(spread[m], mat_y[k], preferred_element_type=F32).astype(BF16)
            acc = acc + lax.dot_general(
                left, spread[m], (((1,), (1,)), ((), ())), preferred_element_type=F32
            )
        lines_y[384 * k : 384 * k + 384, :] = acc.astype(BF16)
    line_to = spots(lax.broadcasted_iota(jnp.int32, (384, 384), 0))[1]
    member_from, line_from = spots(lax.broadcasted_iota(jnp.int32, (384, 384), 1))
    pick = (line_to == line_from) & (member_from == 1)
    lines_y[768:1152, :] = jnp.where(pick, 1.0, 0.0).astype(BF16)


def z_kernel(coef, *refs):
    recv, lines, outs, held, sem = refs[:8], refs[8], refs[9:17], refs[17], refs[18]
    low = low_lanes((192, 128))
    lhs = lines[...]

    def tile(yl, t):
        at = yl * 216 + 24 * t
        return jnp.concatenate([ref[at : at + 24, :].astype(F32) for ref in recv], axis=0)

    def put(t, term):
        for r in range(8):
            held[r, 24 * t : 24 * t + 24, :] = term[24 * r : 24 * r + 24].astype(BF16)

    copies = []

    def ship(n, rows):
        for r in range(8):
            copy = pltpu.make_async_copy(held.at[r, rows], outs[r].at[rows], sem.at[n, r])
            copy.start()
            copies.append(copy)

    tails = []
    for yl in range(3):
        tiles = [tile(yl, t) for t in range(9)]
        vel = tiles[5]
        vel_half = jnp.where(low, swap(tiles[8]), tiles[8])
        names = [0, 1, 2, 3, 4, 6, 7, 8]
        for n in range(0, 8, 2):
            rhs = jnp.concatenate([tiles[names[n]], tiles[names[n + 1]]], axis=1).astype(BF16)
            grad = jnp.dot(lhs, rhs, preferred_element_type=F32)
            for j in range(2):
                t = names[n + j]
                g0 = grad[:192, 128 * j : 128 * j + 128]
                g1 = grad[192:, 128 * j : 128 * j + 128]
                if t < 5:
                    put(yl * 7 + t, coef[t] * g1 - vel * g0)
                elif t < 8:
                    q = t - 6
                    c = jnp.where(low, coef[2 * q], coef[2 * q + 1])
                    put(yl * 7 + 5 + q, c * g1 - vel_half * g0)
                else:
                    tails.append(coef[4] * g1 - vel_half * g0)
        ship(yl, slice(168 * yl, 168 * yl + 168))
    put(21, jnp.where(low, tails[0], swap(tails[1])))
    put(22, jnp.where(low, tails[2], 0.0))
    ship(3, slice(504, 552))
    for copy in copies:
        copy.wait()


def y_kernel(coef, recv, lines, out):
    lhs = lines[0:768, :]
    take = lines[768:1152, :]
    low = low_lanes((384, 128))
    member = lax.broadcasted_iota(jnp.int32, (16, 24, 128), 1).reshape(384, 128) >= 12

    def tile(t):
        return recv[:, 24 * t : 24 * t + 24, :].astype(F32).reshape(384, 128).astype(BF16)

    def put(t, term):
        out[:, 24 * t : 24 * t + 24, :] = term.reshape(16, 24, 128).astype(BF16)

    def coef_of(p):
        if p == 2:
            return jnp.where(member, 0.0, coef[4])
        return jnp.where(member, coef[2 * p + 1], coef[2 * p])

    vel_tail = jnp.dot(
        take, jnp.concatenate([tile(12), tile(13)], axis=1), preferred_element_type=F32
    )
    tail = [vel_tail[:, :128], vel_tail[:, 128:]]
    vel_half = [
        jnp.where(low, tail[0], swap(tail[0])),
        jnp.where(low, swap(tail[0]), tail[0]),
        jnp.where(low, tail[1], swap(tail[1])),
    ]

    work = [(12, tail[0], coef_of(2)), (13, tail[1], coef_of(2))]
    vel_full = jnp.dot(
        take, jnp.concatenate([tile(6), tile(7)], axis=1), preferred_element_type=F32
    )
    vels = [vel_full[:, :128], vel_full[:, 128:]]
    vels.append(jnp.dot(take, tile(8), preferred_element_type=F32))
    for zl in range(3):
        work += [(3 * p + zl, vels[zl], coef_of(p)) for p in range(3)]
        work.append((9 + zl, vel_half[zl], jnp.where(low, coef_of(0), coef_of(1))))
    for n in range(0, 14, 2):
        pair = work[n : n + 2]
        rhs = jnp.concatenate([tile(t) for t, _, _ in pair], axis=1)
        grad = jnp.dot(lhs, rhs, preferred_element_type=F32)
        for k, (t, vel, c) in enumerate(pair):
            lanes = slice(128 * k, 128 * k + 128)
            put(t, c * grad[384:, lanes] - vel * grad[:384, lanes])


CHUNKS = (((6, 7), (7, 0)), ((2, 3), (5, 6)), ((4, 5), (3, 4)), ((0, 1), (1, 2)))


def needs(n):
    return sorted(set(CHUNKS[n][0] + CHUNKS[n][1]))


def group_of(n, me):
    even, odd = CHUNKS[n]
    return lax.rem(me + jnp.where(lax.rem(me, 2) == 0, even[0], odd[0]), 8) // 2


def join_kernel(n, probe, col, *refs):
    base, arrivals = refs[0], dict(zip(needs(n), refs[1:]))
    out, send, own, rows, sem = refs[-5:]
    first = probe[0] == 0
    me = col[0]
    low = low_lanes((24, 128))
    group = group_of(n, me)

    def give(t, half0, half1):
        send[t] = jnp.where(first, half1, half0).astype(BF16)
        own[t] = jnp.where(first, half0, half1).astype(BF16)

    def copy_of(yl):
        return pltpu.make_async_copy(
            rows.at[:, yl], out.at[:, 3 * group + yl], sem.at[yl]
        )

    def fill(pair):
        def z_tile(b, t):
            return arrivals[pair[b]][24 * t : 24 * t + 24, :].astype(F32)

        tails = []
        for yl in range(3):
            y = 3 * group + yl
            mids = []
            for v in range(5):
                full = [z_tile(b, 7 * yl + v) for b in range(2)]
                t, odd = (7 * yl + 5 + v // 2, v % 2) if v < 4 else (21 + yl // 2, yl % 2)
                m = [z_tile(b, t) for b in range(2)]
                if odd:
                    mid = jnp.where(low, swap(m[0]), m[1])
                else:
                    mid = jnp.where(low, m[0], swap(m[1]))
                res = []
                for c, part in enumerate((full[0], mid, full[1])):
                    lanes = slice(128 * c, 128 * c + 128)
                    total = (base[v, y, :, lanes] + step_size * part).astype(BF16)
                    rows[v, yl, :, lanes] = total
                    res.append(total.astype(F32))
                give(5 * yl + v, res[0], res[2])
                mids.append(res[1])
            for q in range(2):
                two = mids[2 * q : 2 * q + 2]
                give(15 + 2 * yl + q, merge(0, *two), merge(1, *two))
            tails.append(mids[4])
            copy_of(yl).start()
        tails.append(jnp.zeros((24, 128), F32))
        for q in range(2):
            two = tails[2 * q : 2 * q + 2]
            give(21 + q, merge(0, *two), merge(1, *two))

    for odd_me in range(2):

        @pl.when(lax.rem(me, 2) == odd_me)
        def _(odd_me=odd_me):
            fill(CHUNKS[n][odd_me])

    for yl in range(3):
        copy_of(yl).wait()


def sketch_kernel(n, probe, col, mix, *refs):
    own, recv = refs[:2]
    out, rows, sem = refs[-3:]
    p = probe[0]
    low = low_lanes((24, 128))
    group = group_of(n, col[0])

    def copy_of(g):
        return pltpu.make_async_copy(rows.at[g], out.at[g, :, pl.ds(3 * group, 3)], sem.at[g])

    def mixed(t, g):
        a = (own[t].astype(F32) * mix[p, g]).astype(BF16).astype(F32)
        b = (recv[t].astype(F32) * mix[1 - p, g]).astype(BF16).astype(F32)
        return a + b

    def put(g, v, yl, full, piece):
        turned = swap(full)
        head = jnp.where(p == 0, full, jnp.where(low, piece, turned))
        tail = jnp.where(p == 0, piece, turned)
        rows[g, v, yl, :, 0:128] = head.astype(BF16)
        rows[g, v, yl, :, 128:192] = tail[:, :64].astype(BF16)

    for g in range(2):
        for yl in range(3):
            for q in range(2):
                half = mixed(15 + 2 * yl + q, g)
                put(g, 2 * q, yl, mixed(5 * yl + 2 * q, g), half)
                put(g, 2 * q + 1, yl, mixed(5 * yl + 2 * q + 1, g), swap(half))
        half = mixed(21, g)
        put(g, 4, 0, mixed(4, g), half)
        put(g, 4, 1, mixed(9, g), swap(half))
        put(g, 4, 2, mixed(14, g), mixed(22, g))
        copy_of(g).start()
    for g in range(2):
        copy_of(g).wait()


def call(kernel, out_shapes, scalars, arrays, scratch=(), kept=(), spaces=None, stay=False):
    many = isinstance(out_shapes, (list, tuple))
    specs = spaces or [vspec() for _ in (out_shapes if many else [0])]
    before = len(scalars) + len(arrays)
    return pl.pallas_call(
        kernel,
        out_shape=out_shapes,
        in_specs=[sspec()] * len(scalars)
        + [pl.BlockSpec(memory_space=pl.ANY) if stay else vspec()] * len(arrays)
        + [pl.BlockSpec(memory_space=pl.ANY)] * len(kept),
        out_specs=specs if many else specs[0],
        scratch_shapes=scratch,
        input_output_aliases={before + n: n for n in range(len(kept))},
        compiler_params=pltpu.CompilerParams(vmem_limit_bytes=16 << 20),
    )(*scalars, *arrays, *kept)


def far(x):
    return pltpu.with_memory_space_constraint(x, pltpu.HBM)


def near(x):
    return pltpu.with_memory_space_constraint(x, pltpu.VMEM)


def shift(x, distance):
    return lax.ppermute(x, "col", [(i, (i + distance) % 8) for i in range(8)])


ROUTES = (3, 5, 4, 2, 6, 1, 7)
RETURNS = (7, 3, 6, 2, 5, 4, 1)
FIRST = 2


def on_device(
    flow_state,
    forcing,
    advect_x,
    advect_y,
    advect_z,
    diffusivity,
    deriv_x,
    deriv_y,
    deriv_z,
    test_mix,
):
    state = flow_state.reshape(5, 12, 24, 384)
    forced = forcing.reshape(5, 12, 24, 384)
    probe = lax.axis_index("probe").astype(jnp.int32).reshape(1)
    col = lax.axis_index("col").astype(jnp.int32).reshape(1)

    def shape(s, t=BF16):
        return jax.ShapeDtypeStruct(s, t)

    def held(s, t=BF16):
        return pltpu.VMEM(s, t)

    def stored(s, t=BF16):
        return pltpu.HBM(s, t)

    any_space = pl.BlockSpec(memory_space=pl.ANY)
    to_y = call(
        y_pack_kernel, [stored((8, 2, 336, 128))], [], [far(state), far(advect_y)],
        [
            pltpu.VMEM((5, 12, 24, 384), BF16),
            pltpu.VMEM((12, 24, 384), BF16),
            pltpu.VMEM((8, 2, 336, 128), BF16),
            pltpu.SemaphoreType.DMA((8,)),
        ],
        stay=True,
        spaces=[any_space],
    )[0]
    at_y = lax.all_to_all(
        to_y.reshape(16, 336, 128), "row", split_axis=0, concat_axis=0, tiled=True
    )
    at_z = {}
    for distances in (ROUTES[:FIRST], (0,) + ROUTES[FIRST:]):
        to_z = call(
            functools.partial(z_pack_kernel, distances),
            [stored((648, 128)) for _ in distances],
            [col],
            [state, advect_z],
            [
                pltpu.VMEM((len(distances), 648, 128), BF16),
                pltpu.SemaphoreType.DMA((len(distances),)),
            ],
            spaces=[any_space] * len(distances),
        )
        for r, piece in zip(distances, to_z):
            at_z[r] = shift(piece, r) if r else piece
    at_z = [at_z[r] for r in range(8)]
    lines_y, lines_z = call(
        matrices_kernel,
        [stored((1152, 384)), stored((384, 192))],
        [col],
        [far(deriv_y), far(deriv_z)],
    )
    term_y = call(y_kernel, stored((16, 336, 128)), [diffusivity], [near(at_y), far(lines_y)])
    back_y = lax.all_to_all(term_y, "row", split_axis=0, concat_axis=0, tiled=True)
    term_z = call(
        z_kernel,
        [stored((552, 128))] * 8,
        [diffusivity],
        [near(x) for x in at_z] + [near(lines_z)],
        [pltpu.VMEM((8, 552, 128), BF16), pltpu.SemaphoreType.DMA((4, 8))],
        spaces=[any_space] * 8,
    )
    back_z = list(term_z)
    for r in RETURNS:
        back_z[r] = shift(term_z[r], -r)
    base = call(
        xy_kernel,
        held((5, 12, 24, 384), F32),
        [diffusivity],
        [state, far(forced), far(advect_x), far(deriv_x), near(back_y.reshape(8, 2, 336, 128))],
        [pltpu.VMEM((24, 24, 384), F32)],
    )
    pieces = [near(x) for x in back_z]
    sections, sketches, halves = [], [], []
    for n in range(4):
        section, send, own = call(
            functools.partial(join_kernel, n),
            [shape((5, 12, 24, 384)), held((23, 24, 128)), held((23, 24, 128))],
            [probe, col],
            [near(base)] + [pieces[r] for r in needs(n)],
            [pltpu.VMEM((5, 3, 24, 384), BF16), pltpu.SemaphoreType.DMA((3,))],
            kept=sections[-1:],
            spaces=[any_space, vspec(), vspec()],
        )
        sections.append(section)
        halves.append((own, lax.ppermute(send, "probe", [(0, 1), (1, 0)])))
    for n in range(4):
        own, recv = halves[n]
        sketches.append(
            call(
                functools.partial(sketch_kernel, n),
                [shape((2, 5, 12, 24, 192))],
                [probe, col, test_mix],
                [near(own), near(recv)],
                [pltpu.VMEM((2, 5, 3, 24, 192), BF16), pltpu.SemaphoreType.DMA((2,))],
                kept=sketches[-1:],
                spaces=[any_space],
            )[0]
        )
    section, sketch = sections[-1], sketches[-1]
    return (section[None], sketch)


def solution(mesh):
    placed = (
        P("probe", None, "row", "col", None),
        P("probe", None, "row", "col", None),
        P("row", "col", None),
        P("row", "col", None),
        P("row", "col", None),
        P(),
        P(),
        P(),
        P(),
        P(),
    )

    return jax.shard_map(
        on_device,
        mesh=mesh,
        in_specs=placed,
        out_specs=(P("probe", None, "row", "col", None), P(None, None, "row", "col", "probe")),
        check_vma=False,
    )
```

```python
import functools

import jax
import jax.numpy as jnp
from jax import lax
from jax.experimental import pallas as pl
from jax.experimental.pallas import tpu as pltpu
from jax.sharding import PartitionSpec as P


step_size = 0.25


F32 = jnp.float32
BF16 = jnp.bfloat16


def vspec():
    return pl.BlockSpec(memory_space=pltpu.VMEM)


def sspec():
    return pl.BlockSpec(memory_space=pltpu.SMEM)


def swap(x):
    return pltpu.roll(x, 64, x.ndim - 1)


def low_lanes(shape):
    return lax.broadcasted_iota(jnp.int32, shape, len(shape) - 1) < 64


def merge(half, first, second):
    low = low_lanes(first.shape)
    if half == 0:
        return jnp.where(low, first, swap(second))
    return jnp.where(low, swap(first), second)


def z_pack_kernel(distances, col, state, adv, *refs):
    me = col[0]
    held, sem = refs[-2:]
    copies = []
    for n, r in enumerate(distances):
        dest = lax.rem(me + r, 8)
        a = dest // 2

        def fill(b, n=n, a=a):
            def body(yl, carry):
                y = 3 * a + yl
                base = pl.multiple_of(yl * 216, 8)
                full = slice(256 * b, 256 * b + 128)
                for u in range(6):
                    src = state[u, y, :, full] if u < 5 else adv[y, :, full]
                    held[n, pl.ds(base + 24 * u, 24), :] = src
                mid = [state[u, y, :, 128:256].astype(F32) for u in range(5)]
                mid.append(adv[y, :, 128:256].astype(F32))
                for q in range(3):
                    tile = merge(b, mid[2 * q], mid[2 * q + 1])
                    held[n, pl.ds(base + 144 + 24 * q, 24), :] = tile.astype(BF16)
                return carry

            lax.fori_loop(0, 3, body, 0)

        @pl.when(lax.rem(dest, 2) == 0)
        def _():
            fill(0)

        @pl.when(lax.rem(dest, 2) == 1)
        def _():
            fill(1)

        copies.append(pltpu.make_async_copy(held.at[n], refs[n], sem.at[n]))
        copies[-1].start()
    for copy in copies:
        copy.wait()


def y_pack_kernel(state_far, adv_far, out_far, state, adv, out, sem):
    copies = [
        pltpu.make_async_copy(state_far.at[0:2], state.at[0:2], sem.at[0]),
        pltpu.make_async_copy(state_far.at[2:4], state.at[2:4], sem.at[1]),
        pltpu.make_async_copy(state_far.at[4], state.at[4], sem.at[2]),
        pltpu.make_async_copy(adv_far, adv, sem.at[3]),
    ]
    for copy in copies:
        copy.start()
    leaving = []

    def ship(n, first, last):
        rows = slice(first, last)
        copy = pltpu.make_async_copy(out.at[:, :, rows], out_far.at[:, :, rows], sem.at[4 + n])
        copy.start()
        leaving.append(copy)

    def lines(p, c):
        lanes = slice(128 * c, 128 * c + 128)
        if p < 2:
            block = state[2 * p : 2 * p + 2, :, :, lanes].astype(F32).reshape(24, 24, 128)
        else:
            block = jnp.concatenate([state[4, :, :, lanes], adv[:, :, lanes]], axis=0).astype(F32)
        return jnp.swapaxes(block, 0, 1)

    for p in range(3):
        for copy in copies[p : p + 1 if p < 2 else 4]:
            copy.wait()
        for b in range(2):
            out[:, b, 72 * p : 72 * p + 72, :] = lines(p, 2 * b).reshape(8, 72, 128).astype(BF16)
        ship(p, 72 * p, 72 * p + 72)
    mid = [lines(p, 1) for p in range(2)]
    for b in range(2):
        tile = merge(b, mid[0], mid[1])
        out[:, b, 216:288, :] = tile.reshape(8, 72, 128).astype(BF16)
    last = lines(2, 1).reshape(8, 3, 24, 128)
    none = jnp.zeros((8, 24, 128), F32)
    for b in range(2):
        out[:, b, 288:312, :] = merge(b, last[:, 0], last[:, 1]).astype(BF16)
        out[:, b, 312:336, :] = merge(b, last[:, 2], none).astype(BF16)
    ship(3, 216, 336)
    for copy in leaving:
        copy.wait()


def xy_kernel(coef, state, forcing, adv, mat, back_y, out, work):
    lhs_mat = mat[...].reshape(768, 384)
    low3 = low_lanes((24, 24, 128))
    low8 = low_lanes((8, 24, 128))

    def put_lines(c, block):
        work[:, :, 128 * c : 128 * c + 128] = jnp.swapaxes(block, 0, 1)

    def y_tile(b, at, n):
        return back_y[:, b, at : at + 24 * n, :].astype(F32)

    for p in range(3):
        for b in range(2):
            put_lines(2 * b, y_tile(b, 72 * p, 3).reshape(24, 24, 128))
        if p < 2:
            m = [y_tile(b, 216, 3).reshape(24, 24, 128) for b in range(2)]
            if p == 0:
                put_lines(1, jnp.where(low3, m[0], swap(m[1])))
            else:
                put_lines(1, jnp.where(low3, swap(m[0]), m[1]))
        else:
            m = [[y_tile(b, 288 + 24 * j, 1) for j in range(2)] for b in range(2)]
            parts = [
                jnp.where(low8, m[0][0], swap(m[1][0])),
                jnp.where(low8, swap(m[0][0]), m[1][0]),
                jnp.where(low8, m[0][1], swap(m[1][1])),
            ]
            put_lines(1, jnp.stack(parts, axis=1).reshape(24, 24, 128))
        for i in range(2 if p < 2 else 1):
            v = 2 * p + i
            for h in range(2):
                ys = slice(6 * h, 6 * h + 6)
                field = state[v, ys].astype(F32).reshape(144, 384)
                grad = lax.dot_general(
                    field.astype(BF16),
                    lhs_mat,
                    (((1,), (1,)), ((), ())),
                    preferred_element_type=F32,
                )
                vel = adv[ys].astype(F32).reshape(144, 384)
                frc = forcing[v, ys].astype(F32).reshape(144, 384)
                term = coef[v] * grad[:, 384:] - vel * grad[:, :384]
                term = term + work[12 * i + 6 * h : 12 * i + 6 * h + 6].reshape(144, 384)
                out[v, ys] = (field + step_size * (term + frc)).reshape(6, 24, 384)


def matrices_kernel(col, mat_y, mat_z, lines_y, lines_z):
    me = col[0]
    point = lax.broadcasted_iota(jnp.int32, (192, 192), 0)
    place = lax.broadcasted_iota(jnp.int32, (192, 192), 1)
    block = jnp.zeros((192, 192), jnp.int32)
    for r in range(8):
        inside = (place >= 24 * r) & (place < 24 * r + 24)
        block = jnp.where(inside, 24 * lax.rem(me - r + 8, 8) - 24 * r, block)
    order = jnp.where(point == place + block, 1.0, 0.0).astype(BF16)
    for k in range(2):
        cols = jnp.dot(mat_z[k], order, preferred_element_type=F32).astype(BF16)
        rows = lax.dot_general(order, cols, (((0,), (0,)), ((), ())), preferred_element_type=F32)
        lines_z[192 * k : 192 * k + 192, :] = rows.astype(BF16)

    def spots(index):
        q = lax.shift_right_logical(index * 5462, 16)
        return lax.rem(q, 2), 12 * lax.shift_right_logical(q, 1) + index - 12 * q

    member, line = spots(lax.broadcasted_iota(jnp.int32, (384, 192), 0))
    same = line == lax.broadcasted_iota(jnp.int32, (384, 192), 1)
    spread = [jnp.where(same & (member == m), 1.0, 0.0).astype(BF16) for m in range(2)]
    for k in range(2):
        acc = jnp.zeros((384, 384), F32)
        for m in range(2):
            left = jnp.dot(spread[m], mat_y[k], preferred_element_type=F32).astype(BF16)
            acc = acc + lax.dot_general(
                left, spread[m], (((1,), (1,)), ((), ())), preferred_element_type=F32
            )
        lines_y[384 * k : 384 * k + 384, :] = acc.astype(BF16)
    line_to = spots(lax.broadcasted_iota(jnp.int32, (384, 384), 0))[1]
    member_from, line_from = spots(lax.broadcasted_iota(jnp.int32, (384, 384), 1))
    pick = (line_to == line_from) & (member_from == 1)
    lines_y[768:1152, :] = jnp.where(pick, 1.0, 0.0).astype(BF16)


def z_kernel(coef, *refs):
    recv, lines, outs, held, sem = refs[:8], refs[8], refs[9:17], refs[17], refs[18]
    low = low_lanes((192, 128))
    lhs = lines[...]

    def tile(yl, t):
        at = yl * 216 + 24 * t
        return jnp.concatenate([ref[at : at + 24, :].astype(F32) for ref in recv], axis=0)

    def put(t, term):
        for r in range(8):
            held[r, 24 * t : 24 * t + 24, :] = term[24 * r : 24 * r + 24].astype(BF16)

    copies = []

    def ship(n, rows):
        for r in range(8):
            copy = pltpu.make_async_copy(held.at[r, rows], outs[r].at[rows], sem.at[n, r])
            copy.start()
            copies.append(copy)

    tails = []
    for yl in range(3):
        tiles = [tile(yl, t) for t in range(9)]
        vel = tiles[5]
        vel_half = jnp.where(low, swap(tiles[8]), tiles[8])
        names = [0, 1, 2, 3, 4, 6, 7, 8]
        for n in range(0, 8, 2):
            rhs = jnp.concatenate([tiles[names[n]], tiles[names[n + 1]]], axis=1).astype(BF16)
            grad = jnp.dot(lhs, rhs, preferred_element_type=F32)
            for j in range(2):
                t = names[n + j]
                g0 = grad[:192, 128 * j : 128 * j + 128]
                g1 = grad[192:, 128 * j : 128 * j + 128]
                if t < 5:
                    put(yl * 7 + t, coef[t] * g1 - vel * g0)
                elif t < 8:
                    q = t - 6
                    c = jnp.where(low, coef[2 * q], coef[2 * q + 1])
                    put(yl * 7 + 5 + q, c * g1 - vel_half * g0)
                else:
                    tails.append(coef[4] * g1 - vel_half * g0)
        ship(yl, slice(168 * yl, 168 * yl + 168))
    put(21, jnp.where(low, tails[0], swap(tails[1])))
    put(22, jnp.where(low, tails[2], 0.0))
    ship(3, slice(504, 552))
    for copy in copies:
        copy.wait()


def y_kernel(coef, recv, lines, out):
    lhs = lines[0:768, :]
    take = lines[768:1152, :]
    low = low_lanes((384, 128))
    member = lax.broadcasted_iota(jnp.int32, (16, 24, 128), 1).reshape(384, 128) >= 12

    def tile(t):
        return recv[:, 24 * t : 24 * t + 24, :].astype(F32).reshape(384, 128).astype(BF16)

    def put(t, term):
        out[:, 24 * t : 24 * t + 24, :] = term.reshape(16, 24, 128).astype(BF16)

    def coef_of(p):
        if p == 2:
            return jnp.where(member, 0.0, coef[4])
        return jnp.where(member, coef[2 * p + 1], coef[2 * p])

    vel_tail = jnp.dot(
        take, jnp.concatenate([tile(12), tile(13)], axis=1), preferred_element_type=F32
    )
    tail = [vel_tail[:, :128], vel_tail[:, 128:]]
    vel_half = [
        jnp.where(low, tail[0], swap(tail[0])),
        jnp.where(low, swap(tail[0]), tail[0]),
        jnp.where(low, tail[1], swap(tail[1])),
    ]

    work = [(12, tail[0], coef_of(2)), (13, tail[1], coef_of(2))]
    vel_full = jnp.dot(
        take, jnp.concatenate([tile(6), tile(7)], axis=1), preferred_element_type=F32
    )
    vels = [vel_full[:, :128], vel_full[:, 128:]]
    vels.append(jnp.dot(take, tile(8), preferred_element_type=F32))
    for zl in range(3):
        work += [(3 * p + zl, vels[zl], coef_of(p)) for p in range(3)]
        work.append((9 + zl, vel_half[zl], jnp.where(low, coef_of(0), coef_of(1))))
    for n in range(0, 14, 2):
        pair = work[n : n + 2]
        rhs = jnp.concatenate([tile(t) for t, _, _ in pair], axis=1)
        grad = jnp.dot(lhs, rhs, preferred_element_type=F32)
        for k, (t, vel, c) in enumerate(pair):
            lanes = slice(128 * k, 128 * k + 128)
            put(t, c * grad[384:, lanes] - vel * grad[:384, lanes])


CHUNKS = (((6, 7), (7, 0)), ((2, 3), (5, 6)), ((4, 5), (3, 4)), ((0, 1), (1, 2)))


def needs(n):
    return sorted(set(CHUNKS[n][0] + CHUNKS[n][1]))


def group_of(n, me):
    even, odd = CHUNKS[n]
    return lax.rem(me + jnp.where(lax.rem(me, 2) == 0, even[0], odd[0]), 8) // 2


def join_kernel(n, probe, col, *refs):
    base, arrivals = refs[0], dict(zip(needs(n), refs[1:]))
    out, send, own, rows, sem = refs[-5:]
    first = probe[0] == 0
    me = col[0]
    low = low_lanes((24, 128))
    group = group_of(n, me)

    def give(t, half0, half1):
        send[t] = jnp.where(first, half1, half0).astype(BF16)
        own[t] = jnp.where(first, half0, half1).astype(BF16)

    def copy_of(yl):
        return pltpu.make_async_copy(
            rows.at[:, yl], out.at[:, 3 * group + yl], sem.at[yl]
        )

    def fill(pair):
        def z_tile(b, t):
            return arrivals[pair[b]][24 * t : 24 * t + 24, :].astype(F32)

        tails = []
        for yl in range(3):
            y = 3 * group + yl
            mids = []
            for v in range(5):
                full = [z_tile(b, 7 * yl + v) for b in range(2)]
                t, odd = (7 * yl + 5 + v // 2, v % 2) if v < 4 else (21 + yl // 2, yl % 2)
                m = [z_tile(b, t) for b in range(2)]
                if odd:
                    mid = jnp.where(low, swap(m[0]), m[1])
                else:
                    mid = jnp.where(low, m[0], swap(m[1]))
                res = []
                for c, part in enumerate((full[0], mid, full[1])):
                    lanes = slice(128 * c, 128 * c + 128)
                    total = (base[v, y, :, lanes] + step_size * part).astype(BF16)
                    rows[v, yl, :, lanes] = total
                    res.append(total.astype(F32))
                give(5 * yl + v, res[0], res[2])
                mids.append(res[1])
            for q in range(2):
                two = mids[2 * q : 2 * q + 2]
                give(15 + 2 * yl + q, merge(0, *two), merge(1, *two))
            tails.append(mids[4])
            copy_of(yl).start()
        tails.append(jnp.zeros((24, 128), F32))
        for q in range(2):
            two = tails[2 * q : 2 * q + 2]
            give(21 + q, merge(0, *two), merge(1, *two))

    for odd_me in range(2):

        @pl.when(lax.rem(me, 2) == odd_me)
        def _(odd_me=odd_me):
            fill(CHUNKS[n][odd_me])

    for yl in range(3):
        copy_of(yl).wait()


def sketch_kernel(chunks, probe, col, mix, *refs):
    out, rows, sem = refs[-3:]
    for k, n in enumerate(chunks):
        own, recv = refs[2 * k : 2 * k + 2]
        sketch_part(n, probe, col, mix, own, recv, out, rows.at[k], sem.at[k])
    for k in range(len(chunks)):
        for g in range(2):
            pltpu.make_async_copy(rows.at[k, g], out.at[g, :, 0:3], sem.at[k, g]).wait()


def sketch_part(n, probe, col, mix, own, recv, out, rows, sem):
    p = probe[0]
    low = low_lanes((24, 128))
    group = group_of(n, col[0])

    def copy_of(g):
        return pltpu.make_async_copy(rows.at[g], out.at[g, :, pl.ds(3 * group, 3)], sem.at[g])

    def mixed(t, g):
        a = (own[t].astype(F32) * mix[p, g]).astype(BF16).astype(F32)
        b = (recv[t].astype(F32) * mix[1 - p, g]).astype(BF16).astype(F32)
        return a + b

    def put(g, v, yl, full, piece):
        turned = swap(full)
        head = jnp.where(p == 0, full, jnp.where(low, piece, turned))
        tail = jnp.where(p == 0, piece, turned)
        rows[g, v, yl, :, 0:128] = head.astype(BF16)
        rows[g, v, yl, :, 128:192] = tail[:, :64].astype(BF16)

    for g in range(2):
        for yl in range(3):
            for q in range(2):
                half = mixed(15 + 2 * yl + q, g)
                put(g, 2 * q, yl, mixed(5 * yl + 2 * q, g), half)
                put(g, 2 * q + 1, yl, mixed(5 * yl + 2 * q + 1, g), swap(half))
        half = mixed(21, g)
        put(g, 4, 0, mixed(4, g), half)
        put(g, 4, 1, mixed(9, g), swap(half))
        put(g, 4, 2, mixed(14, g), mixed(22, g))
        copy_of(g).start()


def call(kernel, out_shapes, scalars, arrays, scratch=(), kept=(), spaces=None, stay=False):
    many = isinstance(out_shapes, (list, tuple))
    specs = spaces or [vspec() for _ in (out_shapes if many else [0])]
    before = len(scalars) + len(arrays)
    return pl.pallas_call(
        kernel,
        out_shape=out_shapes,
        in_specs=[sspec()] * len(scalars)
        + [pl.BlockSpec(memory_space=pl.ANY) if stay else vspec()] * len(arrays)
        + [pl.BlockSpec(memory_space=pl.ANY)] * len(kept),
        out_specs=specs if many else specs[0],
        scratch_shapes=scratch,
        input_output_aliases={before + n: n for n in range(len(kept))},
        compiler_params=pltpu.CompilerParams(vmem_limit_bytes=16 << 20),
    )(*scalars, *arrays, *kept)


def far(x):
    return pltpu.with_memory_space_constraint(x, pltpu.HBM)


def near(x):
    return pltpu.with_memory_space_constraint(x, pltpu.VMEM)


def shift(x, distance):
    return lax.ppermute(x, "col", [(i, (i + distance) % 8) for i in range(8)])


ROUTES = (3, 5, 4, 2, 6, 1, 7)
RETURNS = (7, 3, 6, 2, 5, 4, 1)
FIRST = 2


def on_device(
    flow_state,
    forcing,
    advect_x,
    advect_y,
    advect_z,
    diffusivity,
    deriv_x,
    deriv_y,
    deriv_z,
    test_mix,
):
    state = flow_state.reshape(5, 12, 24, 384)
    forced = forcing.reshape(5, 12, 24, 384)
    probe = lax.axis_index("probe").astype(jnp.int32).reshape(1)
    col = lax.axis_index("col").astype(jnp.int32).reshape(1)

    def shape(s, t=BF16):
        return jax.ShapeDtypeStruct(s, t)

    def held(s, t=BF16):
        return pltpu.VMEM(s, t)

    def stored(s, t=BF16):
        return pltpu.HBM(s, t)

    any_space = pl.BlockSpec(memory_space=pl.ANY)
    to_y = call(
        y_pack_kernel, [stored((8, 2, 336, 128))], [], [far(state), far(advect_y)],
        [
            pltpu.VMEM((5, 12, 24, 384), BF16),
            pltpu.VMEM((12, 24, 384), BF16),
            pltpu.VMEM((8, 2, 336, 128), BF16),
            pltpu.SemaphoreType.DMA((8,)),
        ],
        stay=True,
        spaces=[any_space],
    )[0]
    at_y = lax.all_to_all(
        to_y.reshape(16, 336, 128), "row", split_axis=0, concat_axis=0, tiled=True
    )
    at_z = {}
    for distances in (ROUTES[:FIRST], (0,) + ROUTES[FIRST:]):
        to_z = call(
            functools.partial(z_pack_kernel, distances),
            [stored((648, 128)) for _ in distances],
            [col],
            [state, advect_z],
            [
                pltpu.VMEM((len(distances), 648, 128), BF16),
                pltpu.SemaphoreType.DMA((len(distances),)),
            ],
            spaces=[any_space] * len(distances),
        )
        for r, piece in zip(distances, to_z):
            at_z[r] = shift(piece, r) if r else piece
    at_z = [at_z[r] for r in range(8)]
    lines_y, lines_z = call(
        matrices_kernel,
        [stored((1152, 384)), stored((384, 192))],
        [col],
        [far(deriv_y), far(deriv_z)],
    )
    term_y = call(y_kernel, stored((16, 336, 128)), [diffusivity], [near(at_y), far(lines_y)])
    back_y = lax.all_to_all(term_y, "row", split_axis=0, concat_axis=0, tiled=True)
    term_z = call(
        z_kernel,
        [stored((552, 128))] * 8,
        [diffusivity],
        [near(x) for x in at_z] + [near(lines_z)],
        [pltpu.VMEM((8, 552, 128), BF16), pltpu.SemaphoreType.DMA((4, 8))],
        spaces=[any_space] * 8,
    )
    back_z = list(term_z)
    for r in RETURNS:
        back_z[r] = shift(term_z[r], -r)
    base = call(
        xy_kernel,
        held((5, 12, 24, 384), F32),
        [diffusivity],
        [state, far(forced), far(advect_x), far(deriv_x), near(back_y.reshape(8, 2, 336, 128))],
        [pltpu.VMEM((24, 24, 384), F32)],
    )
    pieces = [near(x) for x in back_z]
    sections, sketches, halves = [], [], []
    for n in range(4):
        section, send, own = call(
            functools.partial(join_kernel, n),
            [shape((5, 12, 24, 384)), held((23, 24, 128)), held((23, 24, 128))],
            [probe, col],
            [near(base)] + [pieces[r] for r in needs(n)],
            [pltpu.VMEM((5, 3, 24, 384), BF16), pltpu.SemaphoreType.DMA((3,))],
            kept=sections[-1:],
            spaces=[any_space, vspec(), vspec()],
        )
        sections.append(section)
        halves.append((own, lax.ppermute(send, "probe", [(0, 1), (1, 0)])))
    for chunks in ((0, 1), (2,), (3,)):
        sketches.append(
            call(
                functools.partial(sketch_kernel, chunks),
                [shape((2, 5, 12, 24, 192))],
                [probe, col, test_mix],
                [near(x) for n in chunks for x in halves[n]],
                [
                    pltpu.VMEM((len(chunks), 2, 5, 3, 24, 192), BF16),
                    pltpu.SemaphoreType.DMA((len(chunks), 2)),
                ],
                kept=sketches[-1:],
                spaces=[any_space],
            )[0]
        )
    section, sketch = sections[-1], sketches[-1]
    return (section[None], sketch)


def solution(mesh):
    placed = (
        P("probe", None, "row", "col", None),
        P("probe", None, "row", "col", None),
        P("row", "col", None),
        P("row", "col", None),
        P("row", "col", None),
        P(),
        P(),
        P(),
        P(),
        P(),
    )

    return jax.shard_map(
        on_device,
        mesh=mesh,
        in_specs=placed,
        out_specs=(P("probe", None, "row", "col", None), P(None, None, "row", "col", "probe")),
        check_vma=False,
    )
```
